128 devices in a mesh: chan: 8 (over y_lo, z), freq: 16 (over y_hi, x, core).
Axes of the slice: x: 4, y: 4 (y_hi: 2, y_lo: 2; y = y_hi * 2 + y_lo), z: 4, core: 2. Of those that a mesh axis runs over, the one named last changes fastest.
Arguments:
- spectra: bfloat16 [2, 32, 256, 1024], P(None, None, 'freq', 'chan'), may hold values from -6 to 6
- block_position: int32 [8], replicated, may hold values from 0 to 7, each once
Outputs:
- taup: float32 [8, 256, 512], P('chan', 'freq')
The draws below stay inside these ranges and needn't reach their ends.
Inputs may be any that keep to these rules, and one draw needn't show every extreme that they name: block_position is a permutation: every fiber position 0 to 7 holds exactly one stored block; group k of the chan axis stores block k.
All inputs are finite; a program needn't handle non-finite values.
Results may differ from the reference program's by a relative error of at most 0.0003.
Values may be sent and summed in bfloat16 or wider, within the bound.
A program may use at most 64 MiB of HBM per device.

```python
import math
import jax
import jax.numpy as jnp
from jax import lax

SEGMENTS = 32
FREQS = 256
BLOCK = 128
GROUP_BLOCKS = 1
SLOWNESS = 256
LAG_TIMES = 512
BLOCKS = 8
CHANNELS = 1024
N_CHAN = 8


def level_of(own_key, shape, shards, low, largest):
    def one(position, parts):
        steps = jax.random.uniform(jax.random.fold_in(jax.random.fold_in(own_key, 6), position), (parts,), jnp.float32, low / len(shards), largest / len(shards))
        return jnp.repeat(jnp.exp(steps), shape[position] // parts).reshape((-1,) + (1,) * (len(shape) - position - 1))

    factor_of = one(*shards[0])
    for cut in shards[1:]:
        factor_of = factor_of * one(*cut)
    return factor_of


def normal_values(stream_key, shape, scale, reach, cuts=(), kind=jnp.bfloat16):
    factor_of = level_of(stream_key, shape, cuts, -0.22, 0.18) if cuts else 1.0
    entries = jax.random.normal(stream_key, shape, jnp.float32) * scale * factor_of
    return jnp.minimum(jnp.maximum(entries, -reach), reach).astype(kind)


def setup_inputs(seed: int = 0) -> dict:
    key_of = jax.random.split(jax.random.key(seed), 3)
    return {
        "spectra": normal_values(key_of[0], (2, SEGMENTS, FREQS, CHANNELS), 1.0, 6.0, ((2, 16), (3, 8))),
        "block_position": jax.random.permutation(key_of[1], BLOCKS).astype(jnp.int32),
    }


def lag_sums(panel):
    leading = panel.shape[:-2]
    extent = panel.shape[-1]
    flat_panel = panel.reshape(leading + (extent * extent,))
    padded = jnp.pad(flat_panel, [(0, 0)] * len(leading) + [(0, extent)])
    skewed = padded.reshape(leading + (extent, extent + 1))
    row_index = lax.broadcasted_iota(jnp.int32, (extent, extent + 1), 0)
    col_index = lax.broadcasted_iota(jnp.int32, (extent, extent + 1), 1)
    before_wrap = row_index + col_index < extent
    forward_lags = lax.optimization_barrier(jnp.sum(jnp.where(before_wrap, skewed, 0.0), axis=-2))
    backward_lags = lax.optimization_barrier(jnp.sum(jnp.where(before_wrap, 0.0, skewed), axis=-2))
    return jnp.concatenate([backward_lags[..., 1:], forward_lags[..., :extent]], axis=-1)

def angles(numerator):
    modulus = 8 * FREQS * BLOCK
    return jnp.mod(numerator, modulus).astype(jnp.float32) * (2.0 * math.pi / modulus)

def inverse_counts(delta_start, delta_count, nblocks):
    deltas = delta_start + lax.broadcasted_iota(jnp.int32, (delta_count, 2 * BLOCK), 0)
    lag_value = lax.broadcasted_iota(jnp.int32, (delta_count, 2 * BLOCK), 1) - BLOCK
    counts = SEGMENTS * (nblocks - deltas) * (BLOCK - jnp.abs(lag_value))
    usable = (lag_value > -BLOCK) & ((deltas >= 1) | (lag_value >= 1))
    inverse = jnp.where(usable, 1.0 / jnp.maximum(counts, 1).astype(jnp.float32), 0.0)
    return jnp.concatenate([inverse, inverse], axis=-1)

def slant_terms(means_block, freq_ids, delta_start, group_blocks):
    bins, delta_count = (means_block.shape[0], means_block.shape[1])
    slow_index = lax.broadcasted_iota(jnp.int32, (1, 1, SLOWNESS), 2) - SLOWNESS // 2
    lag_value = lax.broadcasted_iota(jnp.int32, (1, 2 * BLOCK, 1), 1) - BLOCK
    freq_column = freq_ids.reshape(bins, 1, 1)
    lag_angle = angles(freq_column * slow_index * lag_value)
    cosine = jnp.cos(lag_angle)
    sine_part = jnp.sin(lag_angle)
    lag_table = jnp.concatenate([jnp.concatenate([cosine, sine_part], -1), jnp.concatenate([-sine_part, cosine], -1)], 1)
    rotated = jnp.einsum('fdk,fkp->fdp', means_block, lag_table, precision=lax.Precision.HIGHEST)
    deltas = delta_start + lax.broadcasted_iota(jnp.int32, (1, delta_count, 1), 1)
    offset_angle = angles(freq_column * slow_index * (BLOCK * deltas))
    offset_cos = jnp.cos(offset_angle)
    offset_sin = jnp.sin(offset_angle)
    real_part = rotated[..., :SLOWNESS]
    imag_part = rotated[..., SLOWNESS:]
    shifted_re = real_part * offset_cos - imag_part * offset_sin
    shifted_im = real_part * offset_sin + imag_part * offset_cos
    apertures = delta_count // group_blocks
    summed_re = shifted_re.reshape(bins, apertures, group_blocks, SLOWNESS).sum(axis=2)
    summed_im = shifted_im.reshape(bins, apertures, group_blocks, SLOWNESS).sum(axis=2)
    lag_time = lax.broadcasted_iota(jnp.int32, (1, LAG_TIMES), 1) - LAG_TIMES // 2
    time_angle = angles(freq_ids.reshape(bins, 1) * (4 * BLOCK * lag_time))
    spectrum = jnp.concatenate([summed_re, summed_im], axis=0)
    kernel = jnp.concatenate([jnp.cos(time_angle), -jnp.sin(time_angle)], axis=0)
    result = jnp.einsum('gas,gt->ast', spectrum, kernel, precision=lax.Precision.HIGHEST)
    return result.reshape(apertures * SLOWNESS, LAG_TIMES)

def slant_all(mean_stacks, freq_start, delta_start, group_blocks):
    freq_count, delta_count = (mean_stacks.shape[0], mean_stacks.shape[1])
    block_bins = 4
    block_total = freq_count // block_bins
    blocks = mean_stacks.reshape(block_total, block_bins, delta_count, 4 * BLOCK)
    freq_table = (freq_start + jnp.arange(freq_count, dtype=jnp.int32)).reshape(block_total, block_bins)

    def add_block(running, block_item):
        return (running + slant_terms(block_item[0], block_item[1], delta_start, group_blocks), None)
    initial = jnp.zeros((delta_count // group_blocks * SLOWNESS, LAG_TIMES), jnp.float32)
    summed, unused = lax.scan(add_block, initial, (blocks, freq_table))
    return summed

def cross_of_bin(spectra, freq_id, selector):
    slice_bin = lax.dynamic_index_in_dim(spectra, freq_id, axis=2, keepdims=False).astype(jnp.float32)
    left_side = jnp.concatenate([slice_bin[0], slice_bin[1]], axis=0)
    right_side = jnp.stack([left_side, jnp.concatenate([slice_bin[1], -slice_bin[0]], axis=0)], axis=1)
    cross_block = jnp.einsum('kc,kpd->cpd', left_side, right_side, precision=lax.Precision.HIGHEST)
    nblocks = selector.shape[0]
    panels = cross_block.reshape(nblocks, BLOCK, 2, nblocks, BLOCK).transpose(0, 3, 2, 1, 4)
    lag_block = lag_sums(panels).reshape(nblocks * nblocks, 4 * BLOCK)
    return jnp.dot(selector, lag_block, precision=lax.Precision.HIGHEST)

def reference(spectra, block_position):
    nblocks = block_position.shape[0]
    block_delta = (block_position[None, :] - block_position[:, None]).reshape(1, nblocks * nblocks)
    targets = jnp.arange(nblocks, dtype=jnp.int32)[:, None]
    selector = ((block_delta == targets) & (block_delta >= 0)).astype(jnp.float32)
    stacks = lax.map(lambda freq_id: cross_of_bin(spectra, freq_id, selector), jnp.arange(FREQS, dtype=jnp.int32))
    mean_stacks = stacks * inverse_counts(0, nblocks, nblocks)[None]
    image_term = slant_all(mean_stacks, 0, 0, GROUP_BLOCKS)
    out_scale = math.sqrt(SEGMENTS / (FREQS * GROUP_BLOCKS))
    return (image_term * out_scale).reshape(N_CHAN, SLOWNESS, LAG_TIMES)
```

```python
import functools
import math

import jax
import jax.numpy as jnp
from jax import lax
from jax.experimental import pallas as pl
from jax.experimental.pallas import tpu as pltpu
from jax.sharding import PartitionSpec as P

SEGMENTS = 32
FREQS = 256
BLOCK = 128
SLOWNESS = 256
LAG_TIMES = 512
CHAN = 8
FREQ = 16
BINS = 2
ROWS = 2 * SEGMENTS * BINS
TURN = 8 * FREQS * BLOCK
WIDE = 32
SLABS = SLOWNESS // WIDE
SINE = [(-1) ** k * (2 * math.pi) ** (2 * k + 1) / math.factorial(2 * k + 1) for k in range(7)]


def iota(shape, axis):
    return lax.broadcasted_iota(jnp.int32, shape, axis)


def cosine(steps):
    centered = (steps & (TURN - 1)) - TURN // 2
    turn = jnp.abs(centered).astype(jnp.float32) * (1.0 / TURN) - 0.25
    square = turn * turn
    value = SINE[-1]
    for coefficient in SINE[-2::-1]:
        value = value * square + coefficient
    return value * turn


QUARTER = TURN // 4


def lag_at(place):
    return jnp.where(place < BLOCK, place + 1, place - 2 * BLOCK + 1)


def split(value):
    high = value.astype(jnp.bfloat16)
    low = (value - high.astype(jnp.float32)).astype(jnp.bfloat16)
    return high, low


def dot(left, right):
    return jnp.dot(left, right, preferred_element_type=jnp.float32)


def kernel(
    position_ref,
    spectra_ref,
    out_ref,
    blocks,
    left,
    right,
    weight_cos,
    weight_sin,
    lag_high,
    lag_low,
    time_high,
    time_low,
    terms,
    gathered,
    relayed,
    received,
    turned,
    flipped,
    own_sem,
    send_first,
    recv_first,
    send_second,
    recv_second,
    send_third,
    recv_third,
):
    chan = lax.axis_index("chan")
    freq = lax.axis_index("freq")

    barrier = pltpu.get_barrier_semaphore()
    for step in range(1, CHAN):
        pl.semaphore_signal(
            barrier,
            inc=1,
            device_id={"chan": lax.rem(chan + step, CHAN)},
            device_id_type=pl.DeviceIdType.MESH,
        )
    for step in range(1, FREQ):
        pl.semaphore_signal(
            barrier,
            inc=1,
            device_id={"freq": lax.rem(freq + step, FREQ)},
            device_id_type=pl.DeviceIdType.MESH,
        )
    own = pltpu.make_async_copy(spectra_ref.at[:, chan], blocks.at[chan], own_sem)
    own.start()
    pl.semaphore_wait(barrier, CHAN - 1 + FREQ - 1)

    first = []
    for step in range(1, CHAN):
        peer = lax.rem(chan + step, CHAN)
        copy = pltpu.make_async_remote_copy(
            src_ref=spectra_ref.at[:, peer],
            dst_ref=blocks.at[chan],
            send_sem=send_first.at[step],
            recv_sem=recv_first.at[step],
            device_id={"chan": peer},
            device_id_type=pl.DeviceIdType.MESH,
        )
        copy.start()
        first.append(copy)

    base_bin = 2 * CHAN * freq + 2 * chan

    row = iota((CHAN * SLABS, 2 * BLOCK), 0)
    lane = iota((CHAN * SLABS, 2 * BLOCK), 1)
    offset_bin = row // SLABS
    slow = WIDE * (row % SLABS) - SLOWNESS // 2
    lag = lag_at(lane)
    count = SEGMENTS * (CHAN - offset_bin) * (BLOCK - jnp.abs(lag))
    usable = (jnp.abs(lag) < BLOCK) & ((offset_bin >= 1) | (lag >= 1))
    inverse = jnp.where(usable, 1.0 / jnp.maximum(count, 1).astype(jnp.float32), 0.0)
    for bin_index in range(BINS):
        steps = (base_bin + bin_index) * slow * (BLOCK * offset_bin + lag)
        weight_cos[bin_index] = cosine(steps) * inverse
        weight_sin[bin_index] = cosine(steps - QUARTER) * inverse

    for bin_index in range(BINS):
        row = iota((2 * BLOCK, 2 * BLOCK), 0)
        lane = iota((2 * BLOCK, 2 * BLOCK), 1)
        lag = lag_at(row)
        slow = lane % WIDE
        part = (lane // WIDE) % 2
        lane_bin = (lane // (2 * WIDE)) % BINS
        swapped = lane // (2 * BINS * WIDE)
        steps = (base_bin + bin_index) * slow * lag
        quarter = jnp.where(swapped == 0, -part, 1 - part)
        for row_part in range(2):
            turned_steps = steps + QUARTER * (quarter + row_part)
            table = jnp.where(lane_bin == bin_index, cosine(turned_steps), 0.0)
            high, low = split(table)
            at = pl.ds((2 * bin_index + row_part) * 2 * BLOCK, 2 * BLOCK)
            lag_high[at, :] = high
            lag_low[at, :] = low

    scale = math.sqrt(SEGMENTS / FREQS)
    for bin_index in range(BINS):
        for part in range(2):
            row = iota((CHAN * FREQ, LAG_TIMES), 0)
            time = iota((CHAN * FREQ, LAG_TIMES), 1) - LAG_TIMES // 2
            steps = (2 * row + bin_index) * time * (4 * BLOCK)
            high, low = split(cosine(steps + QUARTER * part) * scale)
            at = pl.ds((2 * bin_index + part) * CHAN * FREQ, CHAN * FREQ)
            time_high[at, :] = high
            time_low[at, :] = low

    own.wait()
    for copy in first:
        copy.wait_recv()

    odd = iota((BLOCK, ROWS), 1) % 2
    mirror = iota((BLOCK, BLOCK), 0) + iota((BLOCK, BLOCK), 1) == BLOCK - 1
    mirror = jnp.where(mirror, 1.0, 0.0).astype(jnp.bfloat16)
    for place in range(CHAN):
        block = jnp.int32(0)
        for index in range(CHAN):
            block = jnp.where(position_ref[index] == place, index, block)
        value = blocks[block].reshape(ROWS, BLOCK)
        half = ROWS // 2
        right[pl.ds(place * ROWS, ROWS), pl.ds(0, BLOCK)] = value
        right[pl.ds(place * ROWS, half), pl.ds(BLOCK, BLOCK)] = value[half:]
        right[pl.ds(place * ROWS + half, half), pl.ds(BLOCK, BLOCK)] = -value[:half]
        across = lax.dot_general(
            mirror, value, (((1,), (1,)), ((), ())), preferred_element_type=jnp.float32
        )
        for bin_index in range(BINS):
            left[pl.ds(bin_index * BLOCK, BLOCK), pl.ds(place * ROWS, ROWS)] = jnp.where(
                odd == bin_index, across, 0.0
            ).astype(jnp.bfloat16)

    wrapped = iota((BLOCK, BLOCK), 0) > iota((BLOCK, BLOCK), 1)
    for delta in range(CHAN):
        depth = (CHAN - delta) * ROWS
        panels = dot(left[:, :depth], right[delta * ROWS :, :])
        sums = []
        for bin_index in range(BINS):
            for part in range(2):
                panel = panels[
                    bin_index * BLOCK : (bin_index + 1) * BLOCK, part * BLOCK : (part + 1) * BLOCK
                ]
                skewed = pltpu.roll(panel, 0, 1, stride=1, stride_axis=0)
                ahead = jnp.sum(jnp.where(wrapped, skewed, 0.0), axis=0, keepdims=True)
                behind = jnp.sum(jnp.where(wrapped, 0.0, skewed), axis=0, keepdims=True)
                sums.append(jnp.concatenate([ahead, behind], axis=1))
        at = pl.ds(delta * SLABS, SLABS)
        pieces = []
        for bin_index in range(BINS):
            real, imag = sums[2 * bin_index], sums[2 * bin_index + 1]
            by_cos = weight_cos[bin_index, at, :]
            by_sin = weight_sin[bin_index, at, :]
            pieces.append(real * by_cos - imag * by_sin)
            pieces.append(real * by_sin + imag * by_cos)
        turned[at, :] = jnp.concatenate(pieces, axis=1)

    high, low = split(turned[...])
    slants = dot(high, lag_high[...]) + dot(low, lag_high[...]) + dot(high, lag_low[...])
    row = iota((CHAN * SLABS, BLOCK), 0)
    lane = iota((CHAN * SLABS, BLOCK), 1)
    steps = (base_bin + lane // (2 * WIDE)) * (lane % WIDE) * (BLOCK * (row // SLABS))
    terms[...] = slants[:, :BLOCK] * cosine(steps) + slants[:, BLOCK:] * cosine(steps - QUARTER)

    second = []
    for step in range(1, CHAN):
        peer = lax.rem(chan + step, CHAN)
        copy = pltpu.make_async_remote_copy(
            src_ref=terms.at[pl.ds(pl.multiple_of(peer * SLABS, SLABS), SLABS), :],
            dst_ref=gathered.at[chan],
            send_sem=send_second.at[step],
            recv_sem=recv_second.at[step],
            device_id={"chan": peer},
            device_id_type=pl.DeviceIdType.MESH,
        )
        copy.start()
        second.append(copy)
    gathered[chan] = terms[pl.ds(pl.multiple_of(chan * SLABS, SLABS), SLABS), :]
    for copy in second:
        copy.wait_recv()

    for slab in range(SLABS):
        relayed[slab] = gathered[:, slab, :]

    third = []
    for step in range(1, FREQ):
        peer = lax.rem(freq + step, FREQ)
        copy = pltpu.make_async_remote_copy(
            src_ref=relayed.at[peer // 2],
            dst_ref=received.at[freq],
            send_sem=send_third.at[step],
            recv_sem=recv_third.at[step],
            device_id={"freq": peer},
            device_id_type=pl.DeviceIdType.MESH,
        )
        copy.start()
        third.append(copy)
    received[freq] = relayed[freq // 2]
    for copy in third:
        copy.wait_recv()

    flipped[...] = received[...].reshape(FREQ * CHAN, BLOCK).T
    half_wide = WIDE // 2
    start = pl.multiple_of(lax.rem(freq, 2) * half_wide, half_wide)
    spectrum = jnp.concatenate(
        [flipped[pl.ds(start + WIDE * index, half_wide), :] for index in range(2 * BINS)],
        axis=1,
    )
    high, low = split(spectrum)
    out_ref[...] = dot(high, time_high[...]) + dot(low, time_high[...]) + dot(high, time_low[...])

    for copy in first + second + third:
        copy.wait_send()


def shards(spectra, block_position):
    pairs = spectra.shape[2] // BINS
    view = spectra.reshape(2 * SEGMENTS, pairs, BINS, BLOCK)
    image = pl.pallas_call(
        kernel,
        out_shape=jax.ShapeDtypeStruct((SLOWNESS // FREQ, LAG_TIMES), jnp.float32),
        in_specs=[
            pl.BlockSpec(memory_space=pltpu.SMEM),
            pl.BlockSpec(memory_space=pl.ANY),
        ],
        out_specs=pl.BlockSpec(memory_space=pltpu.VMEM),
        scratch_shapes=[
            pltpu.VMEM((CHAN, 2 * SEGMENTS, BINS, BLOCK), jnp.bfloat16),
            pltpu.VMEM((BINS * BLOCK, CHAN * ROWS), jnp.bfloat16),
            pltpu.VMEM((CHAN * ROWS, 2 * BLOCK), jnp.bfloat16),
            pltpu.VMEM((BINS, CHAN * SLABS, 2 * BLOCK), jnp.float32),
            pltpu.VMEM((BINS, CHAN * SLABS, 2 * BLOCK), jnp.float32),
            pltpu.VMEM((BINS * 4 * BLOCK, 2 * BLOCK), jnp.bfloat16),
            pltpu.VMEM((BINS * 4 * BLOCK, 2 * BLOCK), jnp.bfloat16),
            pltpu.VMEM((2 * FREQS, LAG_TIMES), jnp.bfloat16),
            pltpu.VMEM((2 * FREQS, LAG_TIMES), jnp.bfloat16),
            pltpu.VMEM((CHAN * SLABS, BLOCK), jnp.float32),
            pltpu.VMEM((CHAN, SLABS, BLOCK), jnp.float32),
            pltpu.VMEM((SLABS, CHAN, BLOCK), jnp.float32),
            pltpu.VMEM((FREQ, CHAN, BLOCK), jnp.float32),
            pltpu.VMEM((CHAN * SLABS, BINS * 4 * BLOCK), jnp.float32),
            pltpu.VMEM((BLOCK, FREQ * CHAN), jnp.float32),
            pltpu.SemaphoreType.DMA,
            pltpu.SemaphoreType.DMA((CHAN,)),
            pltpu.SemaphoreType.DMA((CHAN,)),
            pltpu.SemaphoreType.DMA((CHAN,)),
            pltpu.SemaphoreType.DMA((CHAN,)),
            pltpu.SemaphoreType.DMA((FREQ,)),
            pltpu.SemaphoreType.DMA((FREQ,)),
        ],
        compiler_params=pltpu.CompilerParams(collective_id=0, has_side_effects=True),
        name="slant_stack",
    )(block_position, view)
    return image.reshape(1, image.shape[0], image.shape[1])


def solution(mesh):
    return jax.shard_map(
        shards,
        mesh=mesh,
        in_specs=(P(None, None, "freq", "chan"), P()),
        out_specs=P("chan", "freq", None),
        check_vma=False,
    )
```

```python
import functools
import math

import jax
import jax.numpy as jnp
from jax import lax
from jax.experimental import pallas as pl
from jax.experimental.pallas import tpu as pltpu
from jax.sharding import PartitionSpec as P

SEGMENTS = 32
FREQS = 256
BLOCK = 128
SLOWNESS = 256
LAG_TIMES = 512
CHAN = 8
FREQ = 16
BINS = 2
ROWS = 2 * SEGMENTS * BINS
TURN = 8 * FREQS * BLOCK
WIDE = 32
SLABS = SLOWNESS // WIDE
SINE = [(-1) ** k * (2 * math.pi) ** (2 * k + 1) / math.factorial(2 * k + 1) for k in range(7)]


def iota(shape, axis):
    return lax.broadcasted_iota(jnp.int32, shape, axis)


def cosine(steps):
    centered = (steps & (TURN - 1)) - TURN // 2
    turn = jnp.abs(centered).astype(jnp.float32) * (1.0 / TURN) - 0.25
    square = turn * turn
    value = SINE[-1]
    for coefficient in SINE[-2::-1]:
        value = value * square + coefficient
    return value * turn


QUARTER = TURN // 4


def lag_at(place):
    return jnp.where(place < BLOCK, place + 1, place - 2 * BLOCK + 1)


def split(value):
    high = value.astype(jnp.bfloat16)
    low = (value - high.astype(jnp.float32)).astype(jnp.bfloat16)
    return high, low


def dot(left, right):
    return jnp.dot(left, right, preferred_element_type=jnp.float32)


def kernel(
    position_ref,
    spectra_ref,
    out_ref,
    places,
    blocks,
    left,
    right,
    weight_cos,
    weight_sin,
    lag_high,
    lag_low,
    time_high,
    time_low,
    turned,
    terms,
    received,
    flipped,
    ready,
    place_sem,
    own_sem,
    send_block,
    recv_block,
    send_term,
    recv_term,
):
    chan = lax.axis_index("chan")
    freq = lax.axis_index("freq")

    barrier = pltpu.get_barrier_semaphore()
    for step in range(1, CHAN):
        pl.semaphore_signal(
            barrier,
            inc=1,
            device_id={"chan": lax.rem(chan + step, CHAN)},
            device_id_type=pl.DeviceIdType.MESH,
        )
    for step in range(1, FREQ):
        pl.semaphore_signal(
            barrier,
            inc=1,
            device_id={"freq": lax.rem(freq + step, FREQ)},
            device_id_type=pl.DeviceIdType.MESH,
        )
    own = pltpu.make_async_copy(spectra_ref.at[:, chan], blocks.at[chan], own_sem)
    own.start()
    placing = pltpu.make_async_copy(position_ref, places, place_sem)
    placing.start()
    pl.semaphore_wait(barrier, CHAN - 1 + FREQ - 1)

    arrivals = []
    for step in range(1, CHAN):
        peer = lax.rem(chan + step, CHAN)
        copy = pltpu.make_async_remote_copy(
            src_ref=spectra_ref.at[:, peer],
            dst_ref=blocks.at[chan],
            send_sem=send_block.at[step],
            recv_sem=recv_block.at[step],
            device_id={"chan": peer},
            device_id_type=pl.DeviceIdType.MESH,
        )
        copy.start()
        arrivals.append((step, copy))

    base_bin = 2 * CHAN * freq + 2 * chan

    row = iota((CHAN * SLABS, 2 * BLOCK), 0)
    lane = iota((CHAN * SLABS, 2 * BLOCK), 1)
    offset_bin = row // SLABS
    slow = WIDE * (row % SLABS) - SLOWNESS // 2
    lag = lag_at(lane)
    count = SEGMENTS * (CHAN - offset_bin) * (BLOCK - jnp.abs(lag))
    usable = (jnp.abs(lag) < BLOCK) & ((offset_bin >= 1) | (lag >= 1))
    inverse = jnp.where(usable, 1.0 / jnp.maximum(count, 1).astype(jnp.float32), 0.0)
    for bin_index in range(BINS):
        steps = (base_bin + bin_index) * slow * (BLOCK * offset_bin + lag)
        weight_cos[bin_index] = cosine(steps) * inverse
        weight_sin[bin_index] = cosine(steps - QUARTER) * inverse

    for bin_index in range(BINS):
        row = iota((2 * BLOCK, 2 * BLOCK), 0)
        lane = iota((2 * BLOCK, 2 * BLOCK), 1)
        lag = lag_at(row)
        slow = lane % WIDE
        part = (lane // WIDE) % 2
        lane_bin = (lane // (2 * WIDE)) % BINS
        swapped = lane // (2 * BINS * WIDE)
        steps = (base_bin + bin_index) * slow * lag
        quarter = jnp.where(swapped == 0, -part, 1 - part)
        for row_part in range(2):
            turned_steps = steps + QUARTER * (quarter + row_part)
            table = jnp.where(lane_bin == bin_index, cosine(turned_steps), 0.0)
            high, low = split(table)
            at = pl.ds((2 * bin_index + row_part) * 2 * BLOCK, 2 * BLOCK)
            lag_high[at, :] = high
            lag_low[at, :] = low

    scale = math.sqrt(SEGMENTS / FREQS)
    for bin_index in range(BINS):
        for part in range(2):
            row = iota((CHAN * FREQ, LAG_TIMES), 0)
            time = iota((CHAN * FREQ, LAG_TIMES), 1) - LAG_TIMES // 2
            steps = (2 * row + bin_index) * time * (4 * BLOCK)
            high, low = split(cosine(steps + QUARTER * part) * scale)
            at = pl.ds((2 * bin_index + part) * CHAN * FREQ, CHAN * FREQ)
            time_high[at, :] = high
            time_low[at, :] = low

    odd = iota((BLOCK, ROWS), 1) % 2
    mirror = iota((BLOCK, BLOCK), 0) + iota((BLOCK, BLOCK), 1) == BLOCK - 1
    mirror = jnp.where(mirror, 1.0, 0.0).astype(jnp.bfloat16)
    half = ROWS // 2

    def prepare(index):
        value = blocks[index].reshape(ROWS, BLOCK)
        right[index, :, pl.ds(0, BLOCK)] = value
        right[index, pl.ds(0, half), pl.ds(BLOCK, BLOCK)] = value[half:]
        right[index, pl.ds(half, half), pl.ds(BLOCK, BLOCK)] = -value[:half]
        across = lax.dot_general(
            mirror, value, (((1,), (1,)), ((), ())), preferred_element_type=jnp.float32
        )
        for bin_index in range(BINS):
            left[index, pl.ds(bin_index * BLOCK, BLOCK), :] = jnp.where(
                odd == bin_index, across, 0.0
            ).astype(jnp.bfloat16)

    own.wait()
    prepare(chan)
    for step, copy in arrivals:
        copy.wait_recv()
        prepare(lax.rem(chan - step + CHAN, CHAN))

    for step in range(1, FREQ):
        pl.semaphore_signal(
            ready,
            inc=1,
            device_id={"freq": lax.rem(freq + step, FREQ)},
            device_id_type=pl.DeviceIdType.MESH,
        )

    placing.wait()
    at_place = []
    for place in range(CHAN):
        block = jnp.int32(0)
        for index in range(CHAN):
            block = jnp.where(places[index] == place, index, block)
        at_place.append(block)

    wrapped = iota((BLOCK, BLOCK), 0) > iota((BLOCK, BLOCK), 1)
    for delta in range(CHAN):
        panels = dot(
            jnp.concatenate([left[at_place[place]] for place in range(CHAN - delta)], axis=1),
            jnp.concatenate([right[at_place[place]] for place in range(delta, CHAN)], axis=0),
        )
        sums = []
        for bin_index in range(BINS):
            for part in range(2):
                panel = panels[
                    bin_index * BLOCK : (bin_index + 1) * BLOCK, part * BLOCK : (part + 1) * BLOCK
                ]
                skewed = pltpu.roll(panel, 0, 1, stride=1, stride_axis=0)
                ahead = jnp.sum(jnp.where(wrapped, skewed, 0.0), axis=0, keepdims=True)
                behind = jnp.sum(jnp.where(wrapped, 0.0, skewed), axis=0, keepdims=True)
                sums.append(jnp.concatenate([ahead, behind], axis=1))
        at = pl.ds(delta * SLABS, SLABS)
        pieces = []
        for bin_index in range(BINS):
            real, imag = sums[2 * bin_index], sums[2 * bin_index + 1]
            by_cos = weight_cos[bin_index, at, :]
            by_sin = weight_sin[bin_index, at, :]
            pieces.append(real * by_cos - imag * by_sin)
            pieces.append(real * by_sin + imag * by_cos)
        turned[at, :] = jnp.concatenate(pieces, axis=1)

    high, low = split(turned[...])
    slants = dot(high, lag_high[...]) + dot(low, lag_high[...]) + dot(high, lag_low[...])
    row = iota((CHAN * SLABS, BLOCK), 0)
    lane = iota((CHAN * SLABS, BLOCK), 1)
    steps = (base_bin + lane // (2 * WIDE)) * (lane % WIDE) * (BLOCK * (row // SLABS))
    slants = slants[:, :BLOCK] * cosine(steps) + slants[:, BLOCK:] * cosine(steps - QUARTER)
    terms[...] = slants.reshape(CHAN * SLABS, 1, BLOCK)

    pl.semaphore_wait(ready, FREQ - 1)
    source = freq * CHAN + chan

    def send(step, carry):
        target = lax.rem(chan * FREQ + freq + step, CHAN * FREQ)
        pltpu.make_async_remote_copy(
            src_ref=terms.at[lax.div(target, 2)],
            dst_ref=received.at[source],
            send_sem=send_term,
            recv_sem=recv_term,
            device_id={"chan": lax.div(target, FREQ), "freq": lax.rem(target, FREQ)},
            device_id_type=pl.DeviceIdType.MESH,
        ).start()
        return carry

    others = CHAN * FREQ - 1
    lax.fori_loop(1, others + 1, send, 0, unroll=8)
    received[source] = terms[lax.div(chan * FREQ + freq, 2)]
    everything = received.at[pl.ds(0, others)]
    pltpu.make_async_copy(everything, everything, recv_term).wait()

    flipped[...] = received[...].reshape(FREQ * CHAN, BLOCK).T
    half_wide = WIDE // 2
    start = pl.multiple_of(lax.rem(freq, 2) * half_wide, half_wide)
    spectrum = jnp.concatenate(
        [flipped[pl.ds(start + WIDE * index, half_wide), :] for index in range(2 * BINS)],
        axis=1,
    )
    high, low = split(spectrum)
    out_ref[...] = dot(high, time_high[...]) + dot(low, time_high[...]) + dot(high, time_low[...])

    for step, copy in arrivals:
        copy.wait_send()
    pltpu.make_async_copy(everything, everything, send_term).wait()


def shards(spectra, block_position):
    pairs = spectra.shape[2] // BINS
    view = spectra.reshape(2 * SEGMENTS, pairs, BINS, BLOCK)
    image = pl.pallas_call(
        kernel,
        out_shape=pltpu.VMEM((SLOWNESS // FREQ, LAG_TIMES), jnp.float32),
        in_specs=[
            pl.BlockSpec(memory_space=pl.ANY),
            pl.BlockSpec(memory_space=pl.ANY),
        ],
        out_specs=pl.BlockSpec(memory_space=pltpu.VMEM),
        scratch_shapes=[
            pltpu.SMEM((CHAN,), jnp.int32),
            pltpu.VMEM((CHAN, 2 * SEGMENTS, BINS, BLOCK), jnp.bfloat16),
            pltpu.VMEM((CHAN, BINS * BLOCK, ROWS), jnp.bfloat16),
            pltpu.VMEM((CHAN, ROWS, 2 * BLOCK), jnp.bfloat16),
            pltpu.VMEM((BINS, CHAN * SLABS, 2 * BLOCK), jnp.float32),
            pltpu.VMEM((BINS, CHAN * SLABS, 2 * BLOCK), jnp.float32),
            pltpu.VMEM((BINS * 4 * BLOCK, 2 * BLOCK), jnp.bfloat16),
            pltpu.VMEM((BINS * 4 * BLOCK, 2 * BLOCK), jnp.bfloat16),
            pltpu.VMEM((2 * FREQS, LAG_TIMES), jnp.bfloat16),
            pltpu.VMEM((2 * FREQS, LAG_TIMES), jnp.bfloat16),
            pltpu.VMEM((CHAN * SLABS, BINS * 4 * BLOCK), jnp.float32),
            pltpu.VMEM((CHAN * SLABS, 1, BLOCK), jnp.float32),
            pltpu.VMEM((FREQ * CHAN, 1, BLOCK), jnp.float32),
            pltpu.VMEM((BLOCK, FREQ * CHAN), jnp.float32),
            pltpu.SemaphoreType.REGULAR,
            pltpu.SemaphoreType.DMA,
            pltpu.SemaphoreType.DMA,
            pltpu.SemaphoreType.DMA((CHAN,)),
            pltpu.SemaphoreType.DMA((CHAN,)),
            pltpu.SemaphoreType.DMA,
            pltpu.SemaphoreType.DMA,
        ],
        compiler_params=pltpu.CompilerParams(collective_id=0, has_side_effects=True),
        name="slant_stack",
    )(block_position, view)
    return image.reshape(1, image.shape[0], image.shape[1])


def solution(mesh):
    return jax.shard_map(
        shards,
        mesh=mesh,
        in_specs=(P(None, None, "freq", "chan"), P()),
        out_specs=P("chan", "freq", None),
        check_vma=False,
    )
```

```python
import itertools
import math

import jax
import jax.numpy as jnp
from jax import lax
from jax.experimental import pallas as pl
from jax.experimental.pallas import tpu as pltpu
from jax.sharding import PartitionSpec as P

SEGMENTS = 32
FREQS = 256
BLOCK = 128
SLOWNESS = 256
LAG_TIMES = 512
CHAN = 8
FREQ = 16
BINS = 2
ROWS = 2 * SEGMENTS * BINS
TURN = 8 * FREQS * BLOCK
QUARTER = TURN // 4
WIDE = 32
SLABS = SLOWNESS // WIDE
RING = 4
OFFSETS = ((1, 0), (0, 1), (0, 3), (1, 1), (1, 3), (0, 2), (1, 2))
SEND_ORDER = (0, 1, 2, 3, 4, 5, 6)
WAIT_ORDER = (0, 1, 2, 3, 4, 5, 6)
SINE = [(-1) ** k * (2 * math.pi) ** (2 * k + 1) / math.factorial(2 * k + 1) for k in range(7)]


def hops(offset, chip):
    along_y = (0, 1, 2, 1)[offset[0] + 2 * chip[0]]
    return along_y + min(offset[1], RING - offset[1]) + min(chip[1], RING - chip[1])


FAR_FIRST = sorted(
    (
        (offset, chip, turn)
        for offset in itertools.product(range(2), range(RING))
        for chip in itertools.product(range(2), range(RING))
        for turn in range(2)
        if (offset, chip, turn) != ((0, 0), (0, 0), 0)
    ),
    key=lambda other: -hops(other[0], other[1]),
)


def iota(shape, axis):
    return lax.broadcasted_iota(jnp.int32, shape, axis)


def cosine(steps):
    centered = (steps & (TURN - 1)) - TURN // 2
    turn = jnp.abs(centered).astype(jnp.float32) * (1.0 / TURN) - 0.25
    square = turn * turn
    value = SINE[-1]
    for coefficient in SINE[-2::-1]:
        value = value * square + coefficient
    return value * turn


def lag_at(place):
    return jnp.where(place < BLOCK, place + 1, place - 2 * BLOCK + 1)


def split(value):
    high = value.astype(jnp.bfloat16)
    low = (value - high.astype(jnp.float32)).astype(jnp.bfloat16)
    return high, low


def dot(left, right):
    return jnp.dot(left, right, preferred_element_type=jnp.float32)


def kernel(
    position_ref,
    spectra_ref,
    out_ref,
    places,
    blocks,
    left,
    right,
    weight_cos,
    weight_sin,
    lag_high,
    lag_low,
    time_high,
    time_low,
    turned,
    terms,
    received,
    flipped,
    told_nearby,
    told_along,
    place_sem,
    own_sem,
    send_block,
    recv_block,
    send_term,
    recv_term,
):
    chan = lax.axis_index("chan")
    freq = lax.axis_index("freq")

    ring, spot = lax.div(chan, RING), lax.rem(chan, RING)

    def at_offset(offset):
        return RING * lax.rem(ring + offset[0], 2) + lax.rem(spot + offset[1], RING)

    def signal(semaphore, **target):
        pl.semaphore_signal(
            semaphore, inc=1, device_id=target, device_id_type=pl.DeviceIdType.MESH
        )

    core, over, across = lax.rem(freq, 2), lax.rem(lax.div(freq, 2), RING), lax.div(freq, 8)
    facing = at_offset((1, 0))
    opposite = lax.rem(freq + FREQ // 2, FREQ)
    nearby = (
        {"freq": freq + 1 - 2 * core},
        {"chan": facing, "freq": opposite},
        {"chan": facing, "freq": opposite + 1 - 2 * core},
    )
    along = tuple(
        {"freq": 8 * across + 2 * lax.rem(over + step, RING) + core} for step in (2, 1, 3)
    )

    barrier = pltpu.get_barrier_semaphore()
    for offset in OFFSETS[::-1]:
        signal(barrier, chan=at_offset(offset))
    for other in along + nearby:
        signal(barrier, **other)
    own = pltpu.make_async_copy(spectra_ref.at[:, chan], blocks.at[chan], own_sem)
    own.start()
    placing = pltpu.make_async_copy(position_ref, places, place_sem)
    placing.start()
    pl.semaphore_wait(barrier, len(OFFSETS) + 6)

    arrivals = []
    for step in SEND_ORDER:
        peer = at_offset(OFFSETS[step])
        copy = pltpu.make_async_remote_copy(
            src_ref=spectra_ref.at[:, peer],
            dst_ref=blocks.at[chan],
            send_sem=send_block.at[step],
            recv_sem=recv_block.at[step],
            device_id={"chan": peer},
            device_id_type=pl.DeviceIdType.MESH,
        )
        copy.start()
        arrivals.append((step, copy))
    arrivals.sort(key=lambda arrival: WAIT_ORDER.index(arrival[0]))

    for other in nearby:
        signal(told_nearby, **other)

    base_bin = 2 * CHAN * freq + 2 * chan

    row = iota((CHAN * SLABS, 2 * BLOCK), 0)
    lane = iota((CHAN * SLABS, 2 * BLOCK), 1)
    offset_bin = row // SLABS
    slow = WIDE * (row % SLABS) - SLOWNESS // 2
    lag = lag_at(lane)
    count = SEGMENTS * (CHAN - offset_bin) * (BLOCK - jnp.abs(lag))
    usable = (jnp.abs(lag) < BLOCK) & ((offset_bin >= 1) | (lag >= 1))
    inverse = jnp.where(usable, 1.0 / jnp.maximum(count, 1).astype(jnp.float32), 0.0)
    for bin_index in range(BINS):
        steps = (base_bin + bin_index) * slow * (BLOCK * offset_bin + lag)
        weight_cos[bin_index] = cosine(steps) * inverse
        weight_sin[bin_index] = cosine(steps - QUARTER) * inverse

    for bin_index in range(BINS):
        row = iota((2 * BLOCK, 2 * BLOCK), 0)
        lane = iota((2 * BLOCK, 2 * BLOCK), 1)
        lag = lag_at(row)
        slow = lane % WIDE
        part = (lane // WIDE) % 2
        lane_bin = (lane // (2 * WIDE)) % BINS
        swapped = lane // (2 * BINS * WIDE)
        steps = (base_bin + bin_index) * slow * lag
        quarter = jnp.where(swapped == 0, -part, 1 - part)
        for row_part in range(2):
            turned_steps = steps + QUARTER * (quarter + row_part)
            table = jnp.where(lane_bin == bin_index, cosine(turned_steps), 0.0)
            high, low = split(table)
            at = pl.ds((2 * bin_index + row_part) * 2 * BLOCK, 2 * BLOCK)
            lag_high[at, :] = high
            lag_low[at, :] = low

    pl.semaphore_wait(told_nearby, 3)
    for other in along:
        signal(told_along, **other)

    scale = math.sqrt(SEGMENTS / FREQS)
    for bin_index in range(BINS):
        for part in range(2):
            row = iota((CHAN * FREQ, LAG_TIMES), 0)
            time = iota((CHAN * FREQ, LAG_TIMES), 1) - LAG_TIMES // 2
            steps = (2 * row + bin_index) * time * (4 * BLOCK)
            high, low = split(cosine(steps + QUARTER * part) * scale)
            at = pl.ds((2 * bin_index + part) * CHAN * FREQ, CHAN * FREQ)
            time_high[at, :] = high
            time_low[at, :] = low

    odd = iota((BLOCK, ROWS), 1) % 2
    mirror = iota((BLOCK, BLOCK), 0) + iota((BLOCK, BLOCK), 1) == BLOCK - 1
    mirror = jnp.where(mirror, 1.0, 0.0).astype(jnp.bfloat16)
    half = ROWS // 2

    def prepare(index):
        value = blocks[index].reshape(ROWS, BLOCK)
        right[index, :, pl.ds(0, BLOCK)] = value
        right[index, pl.ds(0, half), pl.ds(BLOCK, BLOCK)] = value[half:]
        right[index, pl.ds(half, half), pl.ds(BLOCK, BLOCK)] = -value[:half]
        across = lax.dot_general(
            mirror, value, (((1,), (1,)), ((), ())), preferred_element_type=jnp.float32
        )
        for bin_index in range(BINS):
            left[index, pl.ds(bin_index * BLOCK, BLOCK), :] = jnp.where(
                odd == bin_index, across, 0.0
            ).astype(jnp.bfloat16)

    own.wait()
    prepare(chan)
    for step, copy in arrivals:
        copy.wait_recv()
        prepare(at_offset((OFFSETS[step][0], RING - OFFSETS[step][1])))

    placing.wait()
    at_place = []
    for place in range(CHAN):
        block = jnp.int32(0)
        for index in range(CHAN):
            block = jnp.where(places[index] == place, index, block)
        at_place.append(block)

    wrapped = iota((BLOCK, BLOCK), 0) > iota((BLOCK, BLOCK), 1)
    for delta in range(CHAN):
        panels = dot(
            jnp.concatenate([left[at_place[place]] for place in range(CHAN - delta)], axis=1),
            jnp.concatenate([right[at_place[place]] for place in range(delta, CHAN)], axis=0),
        )
        sums = []
        for bin_index in range(BINS):
            for part in range(2):
                panel = panels[
                    bin_index * BLOCK : (bin_index + 1) * BLOCK, part * BLOCK : (part + 1) * BLOCK
                ]
                skewed = pltpu.roll(panel, 0, 1, stride=1, stride_axis=0)
                ahead = jnp.sum(jnp.where(wrapped, skewed, 0.0), axis=0, keepdims=True)
                behind = jnp.sum(jnp.where(wrapped, 0.0, skewed), axis=0, keepdims=True)
                sums.append(jnp.concatenate([ahead, behind], axis=1))
        at = pl.ds(delta * SLABS, SLABS)
        pieces = []
        for bin_index in range(BINS):
            real, imag = sums[2 * bin_index], sums[2 * bin_index + 1]
            by_cos = weight_cos[bin_index, at, :]
            by_sin = weight_sin[bin_index, at, :]
            pieces.append(real * by_cos - imag * by_sin)
            pieces.append(real * by_sin + imag * by_cos)
        turned[at, :] = jnp.concatenate(pieces, axis=1)

    high, low = split(turned[...])
    slants = dot(high, lag_high[...]) + dot(low, lag_high[...]) + dot(high, lag_low[...])
    row = iota((CHAN * SLABS, BLOCK), 0)
    lane = iota((CHAN * SLABS, BLOCK), 1)
    steps = (base_bin + lane // (2 * WIDE)) * (lane % WIDE) * (BLOCK * (row // SLABS))
    slants = slants[:, :BLOCK] * cosine(steps) + slants[:, BLOCK:] * cosine(steps - QUARTER)
    terms[...] = slants.reshape(CHAN * SLABS, 1, BLOCK)

    pl.semaphore_wait(told_along, 3)
    source = freq * CHAN + chan
    to_chan = {offset: at_offset(offset) for offset in OFFSETS + ((0, 0),)}
    to_chip = {
        (flip, step): RING * lax.rem(across + flip, 2) + lax.rem(over + step, RING)
        for flip in range(2)
        for step in range(RING)
    }
    to_freq = {
        chip + (turn,): 2 * place + lax.rem(core + turn, 2)
        for chip, place in to_chip.items()
        for turn in range(2)
    }
    for offset, chip, turn in FAR_FIRST:
        pltpu.make_async_remote_copy(
            src_ref=terms.at[to_chan[offset] * SLABS + to_chip[chip]],
            dst_ref=received.at[source],
            send_sem=send_term,
            recv_sem=recv_term,
            device_id={"chan": to_chan[offset], "freq": to_freq[chip + (turn,)]},
            device_id_type=pl.DeviceIdType.MESH,
        ).start()

    others = CHAN * FREQ - 1
    received[source] = terms[lax.div(chan * FREQ + freq, 2)]
    everything = received.at[pl.ds(0, others)]
    pltpu.make_async_copy(everything, everything, recv_term).wait()

    flipped[...] = received[...].reshape(FREQ * CHAN, BLOCK).T
    half_wide = WIDE // 2
    start = pl.multiple_of(lax.rem(freq, 2) * half_wide, half_wide)
    spectrum = jnp.concatenate(
        [flipped[pl.ds(start + WIDE * index, half_wide), :] for index in range(2 * BINS)],
        axis=1,
    )
    high, low = split(spectrum)
    out_ref[...] = dot(high, time_high[...]) + dot(low, time_high[...]) + dot(high, time_low[...])

    for step, copy in arrivals:
        copy.wait_send()
    pltpu.make_async_copy(everything, everything, send_term).wait()


def shards(spectra, block_position):
    pairs = spectra.shape[2] // BINS
    view = spectra.reshape(2 * SEGMENTS, pairs, BINS, BLOCK)
    image = pl.pallas_call(
        kernel,
        out_shape=pltpu.VMEM((SLOWNESS // FREQ, LAG_TIMES), jnp.float32),
        in_specs=[
            pl.BlockSpec(memory_space=pl.ANY),
            pl.BlockSpec(memory_space=pl.ANY),
        ],
        out_specs=pl.BlockSpec(memory_space=pltpu.VMEM),
        scratch_shapes=[
            pltpu.SMEM((CHAN,), jnp.int32),
            pltpu.VMEM((CHAN, 2 * SEGMENTS, BINS, BLOCK), jnp.bfloat16),
            pltpu.VMEM((CHAN, BINS * BLOCK, ROWS), jnp.bfloat16),
            pltpu.VMEM((CHAN, ROWS, 2 * BLOCK), jnp.bfloat16),
            pltpu.VMEM((BINS, CHAN * SLABS, 2 * BLOCK), jnp.float32),
            pltpu.VMEM((BINS, CHAN * SLABS, 2 * BLOCK), jnp.float32),
            pltpu.VMEM((BINS * 4 * BLOCK, 2 * BLOCK), jnp.bfloat16),
            pltpu.VMEM((BINS * 4 * BLOCK, 2 * BLOCK), jnp.bfloat16),
            pltpu.VMEM((2 * FREQS, LAG_TIMES), jnp.bfloat16),
            pltpu.VMEM((2 * FREQS, LAG_TIMES), jnp.bfloat16),
            pltpu.VMEM((CHAN * SLABS, BINS * 4 * BLOCK), jnp.float32),
            pltpu.VMEM((CHAN * SLABS, 1, BLOCK), jnp.float32),
            pltpu.VMEM((FREQ * CHAN, 1, BLOCK), jnp.float32),
            pltpu.VMEM((BLOCK, FREQ * CHAN), jnp.float32),
            pltpu.SemaphoreType.REGULAR,
            pltpu.SemaphoreType.REGULAR,
            pltpu.SemaphoreType.DMA,
            pltpu.SemaphoreType.DMA,
            pltpu.SemaphoreType.DMA((CHAN,)),
            pltpu.SemaphoreType.DMA((CHAN,)),
            pltpu.SemaphoreType.DMA,
            pltpu.SemaphoreType.DMA,
        ],
        compiler_params=pltpu.CompilerParams(collective_id=0, has_side_effects=True),
        name="slant_stack",
    )(block_position, view)
    return image.reshape(1, image.shape[0], image.shape[1])


def solution(mesh):
    return jax.shard_map(
        shards,
        mesh=mesh,
        in_specs=(P(None, None, "freq", "chan"), P()),
        out_specs=P("chan", "freq", None),
        check_vma=False,
    )
```

```python
import itertools
import math

import jax
import jax.numpy as jnp
from jax import lax
from jax.experimental import pallas as pl
from jax.experimental.pallas import tpu as pltpu
from jax.sharding import PartitionSpec as P

SEGMENTS = 32
FREQS = 256
BLOCK = 128
SLOWNESS = 256
LAG_TIMES = 512
CHAN = 8
FREQ = 16
BINS = 2
ROWS = 2 * SEGMENTS * BINS
TURN = 8 * FREQS * BLOCK
QUARTER = TURN // 4
WIDE = 32
SLABS = SLOWNESS // WIDE
RING = 4
OFFSETS = ((1, 0), (0, 1), (0, 3), (1, 1), (1, 3), (0, 2), (1, 2))
WAITS = ((0, 1), (2, 3), (4, 5), (6,))
SINE = [(-1) ** k * (2 * math.pi) ** (2 * k + 1) / math.factorial(2 * k + 1) for k in range(7)]


def hops(offset, chip):
    along_y = (0, 1, 2, 1)[offset[0] + 2 * chip[0]]
    return along_y + min(offset[1], RING - offset[1]) + min(chip[1], RING - chip[1])


FAR_FIRST = sorted(
    (
        (offset, chip, turn)
        for offset in itertools.product(range(2), range(RING))
        for chip in itertools.product(range(2), range(RING))
        for turn in range(2)
        if (offset, chip, turn) != ((0, 0), (0, 0), 0)
    ),
    key=lambda other: -hops(other[0], other[1]),
)


def iota(shape, axis):
    return lax.broadcasted_iota(jnp.int32, shape, axis)


def cosine(steps):
    centered = (steps & (TURN - 1)) - TURN // 2
    turn = jnp.abs(centered).astype(jnp.float32) * (1.0 / TURN) - 0.25
    square = turn * turn
    value = SINE[-1]
    for coefficient in SINE[-2::-1]:
        value = value * square + coefficient
    return value * turn


def lag_at(place):
    return jnp.where(place < BLOCK, place + 1, place - 2 * BLOCK + 1)


def split(value):
    high = value.astype(jnp.bfloat16)
    low = (value - high.astype(jnp.float32)).astype(jnp.bfloat16)
    return high, low


def dot(left, right):
    return jnp.dot(left, right, preferred_element_type=jnp.float32)


def product(left, high, low):
    rows = left.shape[0]
    left_high, left_low = split(left)
    both = dot(jnp.concatenate([left_high, left_low], axis=0), high)
    return both[:rows] + both[rows:] + dot(left_high, low)


def kernel(
    position_ref,
    spectra_ref,
    out_ref,
    places,
    staged,
    blocks,
    left,
    right,
    weight_cos,
    weight_sin,
    lag_high,
    lag_low,
    time_high,
    time_low,
    turned,
    terms,
    received,
    flipped,
    told_nearby,
    told_along,
    place_sem,
    stage_sem,
    send_block,
    recv_block,
    send_term,
    recv_term,
):
    chan = lax.axis_index("chan")
    freq = lax.axis_index("freq")

    ring, spot = lax.div(chan, RING), lax.rem(chan, RING)

    def at_offset(offset):
        return RING * lax.rem(ring + offset[0], 2) + lax.rem(spot + offset[1], RING)

    def signal(semaphore, **target):
        pl.semaphore_signal(
            semaphore, inc=1, device_id=target, device_id_type=pl.DeviceIdType.MESH
        )

    core, over, across = lax.rem(freq, 2), lax.rem(lax.div(freq, 2), RING), lax.div(freq, 8)
    facing = at_offset((1, 0))
    opposite = lax.rem(freq + FREQ // 2, FREQ)
    nearby = (
        {"freq": freq + 1 - 2 * core},
        {"chan": facing, "freq": opposite},
        {"chan": facing, "freq": opposite + 1 - 2 * core},
    )
    along = tuple(
        {"freq": 8 * across + 2 * lax.rem(over + step, RING) + core} for step in (2, 1, 3)
    )

    barrier = pltpu.get_barrier_semaphore()
    for offset in OFFSETS[::-1]:
        signal(barrier, chan=at_offset(offset))
    for other in along + nearby:
        signal(barrier, **other)
    staging = [
        pltpu.make_async_copy(spectra_ref.at[:, index], staged.at[index], stage_sem.at[index])
        for index in range(CHAN)
    ]
    for copy in staging:
        copy.start()
    placing = pltpu.make_async_copy(position_ref, places, place_sem)
    placing.start()
    pl.semaphore_wait(barrier, len(OFFSETS) + 6)

    for copy in staging:
        copy.wait()
    arrivals = []
    for offset in OFFSETS:
        step, peer = len(arrivals), at_offset(offset)
        copy = pltpu.make_async_remote_copy(
            src_ref=staged.at[peer],
            dst_ref=blocks.at[chan],
            send_sem=send_block.at[step],
            recv_sem=recv_block.at[step],
            device_id={"chan": peer},
            device_id_type=pl.DeviceIdType.MESH,
        )
        copy.start()
        arrivals.append(copy)

    for other in nearby:
        signal(told_nearby, **other)

    base_bin = 2 * CHAN * freq + 2 * chan

    row = iota((CHAN * SLABS, 2 * BLOCK), 0)
    lane = iota((CHAN * SLABS, 2 * BLOCK), 1)
    offset_bin = row // SLABS
    slow = WIDE * (row % SLABS) - SLOWNESS // 2
    lag = lag_at(lane)
    count = SEGMENTS * (CHAN - offset_bin) * (BLOCK - jnp.abs(lag))
    usable = (jnp.abs(lag) < BLOCK) & ((offset_bin >= 1) | (lag >= 1))
    inverse = jnp.where(usable, 1.0 / jnp.maximum(count, 1).astype(jnp.float32), 0.0)
    for bin_index in range(BINS):
        steps = (base_bin + bin_index) * slow * (BLOCK * offset_bin + lag)
        weight_cos[bin_index] = cosine(steps) * inverse
        weight_sin[bin_index] = cosine(steps - QUARTER) * inverse

    row = iota((2 * BLOCK, BLOCK), 0)
    lane = iota((2 * BLOCK, BLOCK), 1)
    slow = lane % WIDE
    part = (lane // WIDE) % 2
    for bin_index in range(BINS):
        swapped = (lane < BLOCK // 2) == (bin_index == 1)
        quarter = jnp.where(swapped, 1 - part, -part)
        steps = (base_bin + bin_index) * slow * lag_at(row) + QUARTER * quarter
        for row_part in range(2):
            high, low = split(cosine(steps + QUARTER * row_part))
            at = pl.ds(row_part * 2 * BLOCK, 2 * BLOCK)
            lag_high[bin_index, at, :] = high
            lag_low[bin_index, at, :] = low

    pl.semaphore_wait(told_nearby, 3)
    for other in along:
        signal(told_along, **other)

    scale = math.sqrt(SEGMENTS / FREQS)
    for bin_index in range(BINS):
        for part in range(2):
            row = iota((CHAN * FREQ, LAG_TIMES), 0)
            time = iota((CHAN * FREQ, LAG_TIMES), 1) - LAG_TIMES // 2
            steps = (2 * row + bin_index) * time * (4 * BLOCK)
            high, low = split(cosine(steps + QUARTER * part) * scale)
            at = pl.ds((2 * bin_index + part) * CHAN * FREQ, CHAN * FREQ)
            time_high[at, :] = high
            time_low[at, :] = low

    odd = iota((BLOCK, ROWS), 1) % 2
    mirror = iota((BLOCK, BLOCK), 0) + iota((BLOCK, BLOCK), 1) == BLOCK - 1
    mirror = jnp.where(mirror, 1.0, 0.0).astype(jnp.bfloat16)
    half = ROWS // 2

    def prepare(index, source):
        value = source[index].reshape(ROWS, BLOCK)
        right[index, :, pl.ds(0, BLOCK)] = value
        right[index, pl.ds(0, half), pl.ds(BLOCK, BLOCK)] = value[half:]
        right[index, pl.ds(half, half), pl.ds(BLOCK, BLOCK)] = -value[:half]
        across = lax.dot_general(
            mirror, value, (((1,), (1,)), ((), ())), preferred_element_type=jnp.float32
        )
        for bin_index in range(BINS):
            left[index, pl.ds(bin_index * BLOCK, BLOCK), :] = jnp.where(
                odd == bin_index, across, 0.0
            ).astype(jnp.bfloat16)

    prepare(chan, staged)
    for steps in WAITS:
        for step in steps:
            arrivals[step].wait_recv()
        for step in steps:
            along_y, along_z = OFFSETS[step]
            prepare(at_offset((along_y, RING - along_z)), blocks)

    placing.wait()
    at_place = []
    for place in range(CHAN):
        block = jnp.int32(0)
        for index in range(CHAN):
            block = jnp.where(places[index] == place, index, block)
        at_place.append(block)

    wrapped = iota((BLOCK, BLOCK), 0) > iota((BLOCK, BLOCK), 1)
    for delta in range(CHAN):
        panels = dot(
            jnp.concatenate([left[at_place[place]] for place in range(CHAN - delta)], axis=1),
            jnp.concatenate([right[at_place[place]] for place in range(delta, CHAN)], axis=0),
        )
        sums = []
        for bin_index in range(BINS):
            for part in range(2):
                panel = panels[
                    bin_index * BLOCK : (bin_index + 1) * BLOCK, part * BLOCK : (part + 1) * BLOCK
                ]
                skewed = pltpu.roll(panel, 0, 1, stride=1, stride_axis=0)
                ahead = jnp.sum(jnp.where(wrapped, skewed, 0.0), axis=0, keepdims=True)
                behind = jnp.sum(jnp.where(wrapped, 0.0, skewed), axis=0, keepdims=True)
                sums.append(jnp.concatenate([ahead, behind], axis=1))
        at = pl.ds(delta * SLABS, SLABS)
        pieces = []
        for bin_index in range(BINS):
            real, imag = sums[2 * bin_index], sums[2 * bin_index + 1]
            by_cos = weight_cos[bin_index, at, :]
            by_sin = weight_sin[bin_index, at, :]
            pieces.append(real * by_cos - imag * by_sin)
            pieces.append(real * by_sin + imag * by_cos)
        turned[at, :] = jnp.concatenate(pieces, axis=1)

    by_bin = []
    for bin_index in range(BINS):
        value = turned[:, pl.ds(bin_index * 4 * BLOCK, 4 * BLOCK)]
        by_bin.append(product(value, lag_high[bin_index], lag_low[bin_index]))
    row = iota((CHAN * SLABS, BLOCK), 0)
    lane = iota((CHAN * SLABS, BLOCK), 1)
    first = lane < BLOCK // 2
    plain = jnp.where(first, by_bin[0], by_bin[1])
    swapped = pltpu.roll(jnp.where(first, by_bin[1], by_bin[0]), BLOCK // 2, 1)
    steps = (base_bin + lane // (2 * WIDE)) * (lane % WIDE) * (BLOCK * (row // SLABS))
    slants = plain * cosine(steps) + swapped * cosine(steps - QUARTER)
    terms[...] = slants.reshape(CHAN * SLABS, 1, BLOCK)

    pl.semaphore_wait(told_along, 3)
    source = freq * CHAN + chan
    to_chan = {offset: at_offset(offset) for offset in OFFSETS + ((0, 0),)}
    to_chip = {
        (flip, step): RING * lax.rem(across + flip, 2) + lax.rem(over + step, RING)
        for flip in range(2)
        for step in range(RING)
    }
    to_freq = {
        chip + (turn,): 2 * place + lax.rem(core + turn, 2)
        for chip, place in to_chip.items()
        for turn in range(2)
    }
    for offset, chip, turn in FAR_FIRST:
        pltpu.make_async_remote_copy(
            src_ref=terms.at[to_chan[offset] * SLABS + to_chip[chip]],
            dst_ref=received.at[source],
            send_sem=send_term,
            recv_sem=recv_term,
            device_id={"chan": to_chan[offset], "freq": to_freq[chip + (turn,)]},
            device_id_type=pl.DeviceIdType.MESH,
        ).start()

    others = CHAN * FREQ - 1
    received[source] = terms[lax.div(chan * FREQ + freq, 2)]
    everything = received.at[pl.ds(0, others)]
    pltpu.make_async_copy(everything, everything, recv_term).wait()

    flipped[...] = received[...].reshape(FREQ * CHAN, BLOCK).T
    half_wide = WIDE // 2
    start = pl.multiple_of(lax.rem(freq, 2) * half_wide, half_wide)
    spectrum = jnp.concatenate(
        [flipped[pl.ds(start + WIDE * index, half_wide), :] for index in range(2 * BINS)],
        axis=1,
    )
    out_ref[...] = product(spectrum, time_high[...], time_low[...])

    for copy in arrivals:
        copy.wait_send()
    pltpu.make_async_copy(everything, everything, send_term).wait()


def shards(spectra, block_position):
    pairs = spectra.shape[2] // BINS
    view = spectra.reshape(2 * SEGMENTS, pairs, BINS, BLOCK)
    image = pl.pallas_call(
        kernel,
        out_shape=pltpu.VMEM((SLOWNESS // FREQ, LAG_TIMES), jnp.float32),
        in_specs=[
            pl.BlockSpec(memory_space=pl.ANY),
            pl.BlockSpec(memory_space=pl.ANY),
        ],
        out_specs=pl.BlockSpec(memory_space=pltpu.VMEM),
        scratch_shapes=[
            pltpu.SMEM((CHAN,), jnp.int32),
            pltpu.VMEM((CHAN, 2 * SEGMENTS, BINS, BLOCK), jnp.bfloat16),
            pltpu.VMEM((CHAN, 2 * SEGMENTS, BINS, BLOCK), jnp.bfloat16),
            pltpu.VMEM((CHAN, BINS * BLOCK, ROWS), jnp.bfloat16),
            pltpu.VMEM((CHAN, ROWS, 2 * BLOCK), jnp.bfloat16),
            pltpu.VMEM((BINS, CHAN * SLABS, 2 * BLOCK), jnp.float32),
            pltpu.VMEM((BINS, CHAN * SLABS, 2 * BLOCK), jnp.float32),
            pltpu.VMEM((BINS, 4 * BLOCK, BLOCK), jnp.bfloat16),
            pltpu.VMEM((BINS, 4 * BLOCK, BLOCK), jnp.bfloat16),
            pltpu.VMEM((2 * FREQS, LAG_TIMES), jnp.bfloat16),
            pltpu.VMEM((2 * FREQS, LAG_TIMES), jnp.bfloat16),
            pltpu.VMEM((CHAN * SLABS, BINS * 4 * BLOCK), jnp.float32),
            pltpu.VMEM((CHAN * SLABS, 1, BLOCK), jnp.float32),
            pltpu.VMEM((FREQ * CHAN, 1, BLOCK), jnp.float32),
            pltpu.VMEM((BLOCK, FREQ * CHAN), jnp.float32),
            pltpu.SemaphoreType.REGULAR,
            pltpu.SemaphoreType.REGULAR,
            pltpu.SemaphoreType.DMA,
            pltpu.SemaphoreType.DMA((CHAN,)),
            pltpu.SemaphoreType.DMA((CHAN,)),
            pltpu.SemaphoreType.DMA((CHAN,)),
            pltpu.SemaphoreType.DMA,
            pltpu.SemaphoreType.DMA,
        ],
        compiler_params=pltpu.CompilerParams(collective_id=0, has_side_effects=True),
        name="slant_stack",
    )(block_position, view)
    return image.reshape(1, image.shape[0], image.shape[1])


def solution(mesh):
    return jax.shard_map(
        shards,
        mesh=mesh,
        in_specs=(P(None, None, "freq", "chan"), P()),
        out_specs=P("chan", "freq", None),
        check_vma=False,
    )
```

```python
import itertools
import math

import jax
import jax.numpy as jnp
from jax import lax
from jax.experimental import pallas as pl
from jax.experimental.pallas import tpu as pltpu
from jax.sharding import PartitionSpec as P

SEGMENTS = 32
FREQS = 256
BLOCK = 128
SLOWNESS = 256
LAG_TIMES = 512
CHAN = 8
FREQ = 16
BINS = 2
ROWS = 2 * SEGMENTS * BINS
TURN = 8 * FREQS * BLOCK
QUARTER = TURN // 4
WIDE = 32
SLABS = SLOWNESS // WIDE
RING = 4
OFFSETS = ((1, 0), (0, 1), (0, 3), (1, 1), (1, 3), (0, 2), (1, 2))
WAITS = ((0, 1), (2, 3), (4, 5), (6,))
DELTAS = ((0,), (4, 5, 1, 6, 2, 7, 3))
SINE = [(-1) ** k * (2 * math.pi) ** (2 * k + 1) / math.factorial(2 * k + 1) for k in range(7)]


FAR_FIRST = sorted(
    (
        (chip, turn)
        for chip in itertools.product(range(2), range(RING))
        for turn in range(2)
        if (chip, turn) != ((0, 0), 0)
    ),
    key=lambda other: -other[0][0] - min(other[0][1], RING - other[0][1]),
)


def iota(shape, axis):
    return lax.broadcasted_iota(jnp.int32, shape, axis)


def cosine(steps):
    centered = (steps & (TURN - 1)) - TURN // 2
    turn = jnp.abs(centered).astype(jnp.float32) * (1.0 / TURN) - 0.25
    square = turn * turn
    value = SINE[-1]
    for coefficient in SINE[-2::-1]:
        value = value * square + coefficient
    return value * turn


def lag_at(place):
    return jnp.where(place < BLOCK, place + 1, place - 2 * BLOCK + 1)


def split(value):
    high = value.astype(jnp.bfloat16)
    low = (value - high.astype(jnp.float32)).astype(jnp.bfloat16)
    return high, low


def dot(left, right):
    return jnp.dot(left, right, preferred_element_type=jnp.float32)


def product(left, high, low):
    rows = left.shape[0]
    left_high, left_low = split(left)
    both = dot(jnp.concatenate([left_high, left_low], axis=0), high)
    return both[:rows] + both[rows:] + dot(left_high, low)


def kernel(
    position_ref,
    spectra_ref,
    out_ref,
    places,
    staged,
    blocks,
    left,
    right,
    weight_cos,
    weight_sin,
    lag_high,
    lag_low,
    time_high,
    time_low,
    offset_cos,
    offset_sin,
    turned,
    terms,
    received,
    flipped,
    told_nearby,
    told_along,
    place_sem,
    stage_sem,
    send_block,
    recv_block,
    send_term,
    recv_term,
):
    chan = lax.axis_index("chan")
    freq = lax.axis_index("freq")

    ring, spot = lax.div(chan, RING), lax.rem(chan, RING)

    def at_offset(offset):
        return RING * lax.rem(ring + offset[0], 2) + lax.rem(spot + offset[1], RING)

    def signal(semaphore, **target):
        pl.semaphore_signal(
            semaphore, inc=1, device_id=target, device_id_type=pl.DeviceIdType.MESH
        )

    core, over, across = lax.rem(freq, 2), lax.rem(lax.div(freq, 2), RING), lax.div(freq, 8)
    facing = at_offset((1, 0))
    opposite = lax.rem(freq + FREQ // 2, FREQ)
    nearby = (
        {"freq": freq + 1 - 2 * core},
        {"chan": facing, "freq": opposite},
        {"chan": facing, "freq": opposite + 1 - 2 * core},
    )
    along = tuple(
        {"freq": 8 * across + 2 * lax.rem(over + step, RING) + core} for step in (2, 1, 3)
    )

    barrier = pltpu.get_barrier_semaphore()
    for offset in OFFSETS[::-1]:
        signal(barrier, chan=at_offset(offset))
    for other in along + nearby:
        signal(barrier, **other)
    staging = [
        pltpu.make_async_copy(spectra_ref.at[:, index], staged.at[index], stage_sem.at[index])
        for index in range(CHAN)
    ]
    for copy in staging:
        copy.start()
    placing = pltpu.make_async_copy(position_ref, places, place_sem)
    placing.start()
    pl.semaphore_wait(barrier, len(OFFSETS) + 6)

    for copy in staging:
        copy.wait()
    arrivals = []
    for offset in OFFSETS:
        step, peer = len(arrivals), at_offset(offset)
        copy = pltpu.make_async_remote_copy(
            src_ref=staged.at[peer],
            dst_ref=blocks.at[chan],
            send_sem=send_block.at[step],
            recv_sem=recv_block.at[step],
            device_id={"chan": peer},
            device_id_type=pl.DeviceIdType.MESH,
        )
        copy.start()
        arrivals.append(copy)

    for other in nearby:
        signal(told_nearby, **other)

    base_bin = 2 * CHAN * freq + 2 * chan

    row = iota((CHAN * SLABS, 2 * BLOCK), 0)
    lane = iota((CHAN * SLABS, 2 * BLOCK), 1)
    offset_bin = row // SLABS
    slow = WIDE * (row % SLABS) - SLOWNESS // 2
    lag = lag_at(lane)
    count = SEGMENTS * (CHAN - offset_bin) * (BLOCK - jnp.abs(lag))
    usable = (jnp.abs(lag) < BLOCK) & ((offset_bin >= 1) | (lag >= 1))
    inverse = jnp.where(usable, 1.0 / jnp.maximum(count, 1).astype(jnp.float32), 0.0)
    for bin_index in range(BINS):
        steps = (base_bin + bin_index) * slow * (BLOCK * offset_bin + lag)
        weight_cos[bin_index] = cosine(steps) * inverse
        weight_sin[bin_index] = cosine(steps - QUARTER) * inverse

    row = iota((CHAN * SLABS, BLOCK), 0)
    lane = iota((CHAN * SLABS, BLOCK), 1)
    steps = (base_bin + lane // (2 * WIDE)) * (lane % WIDE) * (BLOCK * (row // SLABS))
    offset_cos[...] = cosine(steps)
    offset_sin[...] = cosine(steps - QUARTER)

    row = iota((2 * BLOCK, BLOCK), 0)
    lane = iota((2 * BLOCK, BLOCK), 1)
    slow = lane % WIDE
    part = (lane // WIDE) % 2
    for bin_index in range(BINS):
        swapped = (lane < BLOCK // 2) == (bin_index == 1)
        quarter = jnp.where(swapped, 1 - part, -part)
        steps = (base_bin + bin_index) * slow * lag_at(row) + QUARTER * quarter
        for row_part in range(2):
            high, low = split(cosine(steps + QUARTER * row_part))
            at = pl.ds(row_part * 2 * BLOCK, 2 * BLOCK)
            lag_high[bin_index, at, :] = high
            lag_low[bin_index, at, :] = low

    pl.semaphore_wait(told_nearby, 3)
    for other in along:
        signal(told_along, **other)

    scale = math.sqrt(SEGMENTS / FREQS)
    for bin_index in range(BINS):
        for part in range(2):
            row = iota((CHAN * FREQ, LAG_TIMES), 0)
            time = iota((CHAN * FREQ, LAG_TIMES), 1) - LAG_TIMES // 2
            steps = (2 * row + bin_index) * time * (4 * BLOCK)
            high, low = split(cosine(steps + QUARTER * part) * scale)
            at = pl.ds((2 * bin_index + part) * CHAN * FREQ, CHAN * FREQ)
            time_high[at, :] = high
            time_low[at, :] = low

    odd = iota((BLOCK, ROWS), 1) % 2
    mirror = iota((BLOCK, BLOCK), 0) + iota((BLOCK, BLOCK), 1) == BLOCK - 1
    mirror = jnp.where(mirror, 1.0, 0.0).astype(jnp.bfloat16)
    half = ROWS // 2

    def prepare(index, source):
        value = source[index].reshape(ROWS, BLOCK)
        right[index, :, pl.ds(0, BLOCK)] = value
        right[index, pl.ds(0, half), pl.ds(BLOCK, BLOCK)] = value[half:]
        right[index, pl.ds(half, half), pl.ds(BLOCK, BLOCK)] = -value[:half]
        across = lax.dot_general(
            mirror, value, (((1,), (1,)), ((), ())), preferred_element_type=jnp.float32
        )
        for bin_index in range(BINS):
            left[index, pl.ds(bin_index * BLOCK, BLOCK), :] = jnp.where(
                odd == bin_index, across, 0.0
            ).astype(jnp.bfloat16)

    prepare(chan, staged)
    for steps in WAITS:
        for step in steps:
            arrivals[step].wait_recv()
        for step in steps:
            along_y, along_z = OFFSETS[step]
            prepare(at_offset((along_y, RING - along_z)), blocks)

    placing.wait()
    at_place = []
    for place in range(CHAN):
        block = jnp.int32(0)
        for index in range(CHAN):
            block = jnp.where(places[index] == place, index, block)
        at_place.append(block)

    wrapped = iota((BLOCK, BLOCK), 0) > iota((BLOCK, BLOCK), 1)

    def lag_terms(delta):
        panels = dot(
            jnp.concatenate([left[at_place[place]] for place in range(CHAN - delta)], axis=1),
            jnp.concatenate([right[at_place[place]] for place in range(delta, CHAN)], axis=0),
        )
        sums = []
        for bin_index in range(BINS):
            for part in range(2):
                panel = panels[
                    bin_index * BLOCK : (bin_index + 1) * BLOCK, part * BLOCK : (part + 1) * BLOCK
                ]
                skewed = pltpu.roll(panel, 0, 1, stride=1, stride_axis=0)
                ahead = jnp.sum(jnp.where(wrapped, skewed, 0.0), axis=0, keepdims=True)
                behind = jnp.sum(jnp.where(wrapped, 0.0, skewed), axis=0, keepdims=True)
                sums.append(jnp.concatenate([ahead, behind], axis=1))
        at = pl.ds(delta * SLABS, SLABS)
        for bin_index in range(BINS):
            real, imag = sums[2 * bin_index], sums[2 * bin_index + 1]
            by_cos = weight_cos[bin_index, at, :]
            by_sin = weight_sin[bin_index, at, :]
            turned[bin_index, at, pl.ds(0, 2 * BLOCK)] = real * by_cos - imag * by_sin
            turned[bin_index, at, pl.ds(2 * BLOCK, 2 * BLOCK)] = real * by_sin + imag * by_cos

    def slant_terms(deltas):
        rows = [pl.ds(delta * SLABS, SLABS) for delta in deltas]
        by_bin = [
            product(
                jnp.concatenate([turned[bin_index, at, :] for at in rows], axis=0),
                lag_high[bin_index],
                lag_low[bin_index],
            )
            for bin_index in range(BINS)
        ]
        first = iota(by_bin[0].shape, 1) < BLOCK // 2
        plain = jnp.where(first, by_bin[0], by_bin[1])
        swapped = pltpu.roll(jnp.where(first, by_bin[1], by_bin[0]), BLOCK // 2, 1)
        for index, at in enumerate(rows):
            part = slice(index * SLABS, (index + 1) * SLABS)
            slants = plain[part] * offset_cos[at, :] + swapped[part] * offset_sin[at, :]
            terms[at] = slants.reshape(SLABS, 1, BLOCK)

    source = freq * CHAN + chan
    to_chip = {
        (flip, step): RING * lax.rem(across + flip, 2) + lax.rem(over + step, RING)
        for flip in range(2)
        for step in range(RING)
    }
    to_freq = {
        chip + (turn,): 2 * place + lax.rem(core + turn, 2)
        for chip, place in to_chip.items()
        for turn in range(2)
    }

    def post(delta, chip, turn):
        pltpu.make_async_remote_copy(
            src_ref=terms.at[delta * SLABS + to_chip[chip]],
            dst_ref=received.at[source],
            send_sem=send_term,
            recv_sem=recv_term,
            device_id={"chan": delta, "freq": to_freq[chip + (turn,)]},
            device_id_type=pl.DeviceIdType.MESH,
        ).start()

    def post_all(delta):
        for chip, turn in FAR_FIRST:
            post(delta, chip, turn)

        @pl.when(chan != delta)
        def _():
            post(delta, (0, 0), 0)

    for deltas in DELTAS:
        for delta in deltas:
            lag_terms(delta)
        slant_terms(deltas)
        if deltas == DELTAS[0]:
            pl.semaphore_wait(told_along, 3)
        for delta in deltas:
            post_all(delta)

    others = CHAN * FREQ - 1
    received[source] = terms[lax.div(chan * FREQ + freq, 2)]
    everything = received.at[pl.ds(0, others)]
    pltpu.make_async_copy(everything, everything, recv_term).wait()

    flipped[...] = received[...].reshape(FREQ * CHAN, BLOCK).T
    half_wide = WIDE // 2
    start = pl.multiple_of(lax.rem(freq, 2) * half_wide, half_wide)
    spectrum = jnp.concatenate(
        [flipped[pl.ds(start + WIDE * index, half_wide), :] for index in range(2 * BINS)],
        axis=1,
    )
    out_ref[...] = product(spectrum, time_high[...], time_low[...])

    for copy in arrivals:
        copy.wait_send()
    pltpu.make_async_copy(everything, everything, send_term).wait()


def shards(spectra, block_position):
    pairs = spectra.shape[2] // BINS
    view = spectra.reshape(2 * SEGMENTS, pairs, BINS, BLOCK)
    image = pl.pallas_call(
        kernel,
        out_shape=pltpu.VMEM((SLOWNESS // FREQ, LAG_TIMES), jnp.float32),
        in_specs=[
            pl.BlockSpec(memory_space=pl.ANY),
            pl.BlockSpec(memory_space=pl.ANY),
        ],
        out_specs=pl.BlockSpec(memory_space=pltpu.VMEM),
        scratch_shapes=[
            pltpu.SMEM((CHAN,), jnp.int32),
            pltpu.VMEM((CHAN, 2 * SEGMENTS, BINS, BLOCK), jnp.bfloat16),
            pltpu.VMEM((CHAN, 2 * SEGMENTS, BINS, BLOCK), jnp.bfloat16),
            pltpu.VMEM((CHAN, BINS * BLOCK, ROWS), jnp.bfloat16),
            pltpu.VMEM((CHAN, ROWS, 2 * BLOCK), jnp.bfloat16),
            pltpu.VMEM((BINS, CHAN * SLABS, 2 * BLOCK), jnp.float32),
            pltpu.VMEM((BINS, CHAN * SLABS, 2 * BLOCK), jnp.float32),
            pltpu.VMEM((BINS, 4 * BLOCK, BLOCK), jnp.bfloat16),
            pltpu.VMEM((BINS, 4 * BLOCK, BLOCK), jnp.bfloat16),
            pltpu.VMEM((2 * FREQS, LAG_TIMES), jnp.bfloat16),
            pltpu.VMEM((2 * FREQS, LAG_TIMES), jnp.bfloat16),
            pltpu.VMEM((CHAN * SLABS, BLOCK), jnp.float32),
            pltpu.VMEM((CHAN * SLABS, BLOCK), jnp.float32),
            pltpu.VMEM((BINS, CHAN * SLABS, 4 * BLOCK), jnp.float32),
            pltpu.VMEM((CHAN * SLABS, 1, BLOCK), jnp.float32),
            pltpu.VMEM((FREQ * CHAN, 1, BLOCK), jnp.float32),
            pltpu.VMEM((BLOCK, FREQ * CHAN), jnp.float32),
            pltpu.SemaphoreType.REGULAR,
            pltpu.SemaphoreType.REGULAR,
            pltpu.SemaphoreType.DMA,
            pltpu.SemaphoreType.DMA((CHAN,)),
            pltpu.SemaphoreType.DMA((CHAN,)),
            pltpu.SemaphoreType.DMA((CHAN,)),
            pltpu.SemaphoreType.DMA,
            pltpu.SemaphoreType.DMA,
        ],
        compiler_params=pltpu.CompilerParams(collective_id=0, has_side_effects=True),
        name="slant_stack",
    )(block_position, view)
    return image.reshape(1, image.shape[0], image.shape[1])


def solution(mesh):
    return jax.shard_map(
        shards,
        mesh=mesh,
        in_specs=(P(None, None, "freq", "chan"), P()),
        out_specs=P("chan", "freq", None),
        check_vma=False,
    )
```

```python
import itertools
import math

import jax
import jax.numpy as jnp
from jax import lax
from jax.experimental import pallas as pl
from jax.experimental.pallas import tpu as pltpu
from jax.sharding import PartitionSpec as P

SEGMENTS = 32
FREQS = 256
BLOCK = 128
SLOWNESS = 256
LAG_TIMES = 512
CHAN = 8
FREQ = 16
BINS = 2
ROWS = 2 * SEGMENTS * BINS
TURN = 8 * FREQS * BLOCK
QUARTER = TURN // 4
WIDE = 32
SLABS = SLOWNESS // WIDE
RING = 4
OFFSETS = ((1, 0), (0, 1), (0, 3), (1, 1), (1, 3), (0, 2), (1, 2))
WAITS = ((0, 1), (2, 3), (4, 5), (6,))
ALL = True
DELTAS = ((0,), (4, 5, 1, 6, 2, 7, 3))
SINE = [(-1) ** k * (2 * math.pi) ** (2 * k + 1) / math.factorial(2 * k + 1) for k in range(7)]


FAR_FIRST = sorted(
    (
        (chip, turn)
        for chip in itertools.product(range(2), range(RING))
        for turn in range(2)
        if (chip, turn) != ((0, 0), 0)
    ),
    key=lambda other: -other[0][0] - min(other[0][1], RING - other[0][1]),
)


def iota(shape, axis):
    return lax.broadcasted_iota(jnp.int32, shape, axis)


def cosine(steps):
    centered = (steps & (TURN - 1)) - TURN // 2
    turn = jnp.abs(centered).astype(jnp.float32) * (1.0 / TURN) - 0.25
    square = turn * turn
    value = SINE[-1]
    for coefficient in SINE[-2::-1]:
        value = value * square + coefficient
    return value * turn


def lag_at(place):
    return jnp.where(place < BLOCK, place + 1, place - 2 * BLOCK + 1)


def split(value):
    high = value.astype(jnp.bfloat16)
    low = (value - high.astype(jnp.float32)).astype(jnp.bfloat16)
    return high, low


def dot(left, right):
    return jnp.dot(left, right, preferred_element_type=jnp.float32)


def product(left, high, low):
    rows = left.shape[0]
    left_high, left_low = split(left)
    both = dot(jnp.concatenate([left_high, left_low], axis=0), high)
    return both[:rows] + both[rows:] + dot(left_high, low)


def kernel(
    position_ref,
    spectra_ref,
    out_ref,
    places,
    staged,
    blocks,
    left,
    right,
    weight_cos,
    weight_sin,
    lag_high,
    lag_low,
    time_high,
    time_low,
    offset_cos,
    offset_sin,
    square,
    turned,
    terms,
    received,
    flipped,
    told_nearby,
    told_along,
    place_sem,
    stage_sem,
    send_block,
    recv_block,
    send_term,
    recv_term,
):
    chan = lax.axis_index("chan")
    freq = lax.axis_index("freq")

    ring, spot = lax.div(chan, RING), lax.rem(chan, RING)

    def at_offset(offset):
        return RING * lax.rem(ring + offset[0], 2) + lax.rem(spot + offset[1], RING)

    def signal(semaphore, **target):
        pl.semaphore_signal(
            semaphore, inc=1, device_id=target, device_id_type=pl.DeviceIdType.MESH
        )

    core, over, across = lax.rem(freq, 2), lax.rem(lax.div(freq, 2), RING), lax.div(freq, 8)
    facing = at_offset((1, 0))
    opposite = lax.rem(freq + FREQ // 2, FREQ)
    nearby = (
        {"freq": freq + 1 - 2 * core},
        {"chan": facing, "freq": opposite},
        {"chan": facing, "freq": opposite + 1 - 2 * core},
    )
    along = tuple(
        {"freq": 8 * across + 2 * lax.rem(over + step, RING) + core} for step in (2, 1, 3)
    )

    barrier = pltpu.get_barrier_semaphore()
    for offset in OFFSETS[::-1]:
        signal(barrier, chan=at_offset(offset))
    for other in along + nearby:
        signal(barrier, **other)
    staging = [
        pltpu.make_async_copy(spectra_ref.at[:, index], staged.at[index], stage_sem.at[index])
        for index in range(CHAN)
    ]
    for copy in staging:
        copy.start()
    placing = pltpu.make_async_copy(position_ref, places, place_sem)
    placing.start()
    pl.semaphore_wait(barrier, len(OFFSETS) + 6)

    for copy in staging:
        copy.wait()
    arrivals = []
    for offset in OFFSETS:
        step, peer = len(arrivals), at_offset(offset)
        copy = pltpu.make_async_remote_copy(
            src_ref=staged.at[peer],
            dst_ref=blocks.at[chan],
            send_sem=send_block.at[step],
            recv_sem=recv_block.at[step],
            device_id={"chan": peer},
            device_id_type=pl.DeviceIdType.MESH,
        )
        copy.start()
        arrivals.append(copy)

    for other in nearby:
        signal(told_nearby, **other)

    base_bin = 2 * CHAN * freq + 2 * chan

    row = iota((CHAN * SLABS, 2 * BLOCK), 0)
    lane = iota((CHAN * SLABS, 2 * BLOCK), 1)
    offset_bin = row // SLABS
    slow = WIDE * (row % SLABS) - SLOWNESS // 2
    lag = lag_at(lane)
    count = SEGMENTS * (CHAN - offset_bin) * (BLOCK - jnp.abs(lag))
    usable = (jnp.abs(lag) < BLOCK) & ((offset_bin >= 1) | (lag >= 1))
    inverse = jnp.where(usable, 1.0 / jnp.maximum(count, 1).astype(jnp.float32), 0.0)
    for bin_index in range(BINS):
        steps = (base_bin + bin_index) * slow * (BLOCK * offset_bin + lag)
        weight_cos[bin_index] = cosine(steps) * inverse
        weight_sin[bin_index] = cosine(steps - QUARTER) * inverse

    row = iota((CHAN * SLABS, BLOCK), 0)
    lane = iota((CHAN * SLABS, BLOCK), 1)
    steps = (base_bin + lane // (2 * WIDE)) * (lane % WIDE) * (BLOCK * (row // SLABS))
    offset_cos[...] = cosine(steps)
    offset_sin[...] = cosine(steps - QUARTER)

    row = iota((2 * BLOCK, BLOCK), 0)
    lane = iota((2 * BLOCK, BLOCK), 1)
    slow = lane % WIDE
    part = (lane // WIDE) % 2
    for bin_index in range(BINS):
        swapped = (lane < BLOCK // 2) == (bin_index == 1)
        quarter = jnp.where(swapped, 1 - part, -part)
        steps = (base_bin + bin_index) * slow * lag_at(row) + QUARTER * quarter
        for row_part in range(2):
            high, low = split(cosine(steps + QUARTER * row_part))
            at = pl.ds(row_part * 2 * BLOCK, 2 * BLOCK)
            lag_high[bin_index, at, :] = high
            lag_low[bin_index, at, :] = low

    pl.semaphore_wait(told_nearby, 3)
    for other in along:
        signal(told_along, **other)

    scale = math.sqrt(SEGMENTS / FREQS)
    for bin_index in range(BINS):
        for part in range(2):
            row = iota((CHAN * FREQ, LAG_TIMES), 0)
            time = iota((CHAN * FREQ, LAG_TIMES), 1) - LAG_TIMES // 2
            steps = (2 * row + bin_index) * time * (4 * BLOCK)
            high, low = split(cosine(steps + QUARTER * part) * scale)
            at = pl.ds((2 * bin_index + part) * CHAN * FREQ, CHAN * FREQ)
            time_high[at, :] = high
            time_low[at, :] = low

    odd = iota((BLOCK, ROWS), 1) % 2
    mirror = iota((BLOCK, BLOCK), 0) + iota((BLOCK, BLOCK), 1) == BLOCK - 1
    mirror = jnp.where(mirror, 1.0, 0.0).astype(jnp.bfloat16)
    half = ROWS // 2

    def prepare(index, source):
        value = source[index].reshape(ROWS, BLOCK)
        right[index, :, pl.ds(0, BLOCK)] = value
        right[index, pl.ds(0, half), pl.ds(BLOCK, BLOCK)] = value[half:]
        right[index, pl.ds(half, half), pl.ds(BLOCK, BLOCK)] = -value[:half]
        across = lax.dot_general(
            mirror, value, (((1,), (1,)), ((), ())), preferred_element_type=jnp.float32
        )
        for bin_index in range(BINS):
            left[index, pl.ds(bin_index * BLOCK, BLOCK), :] = jnp.where(
                odd == bin_index, across, 0.0
            ).astype(jnp.bfloat16)

    def paired(indices):
        return dot(
            jnp.concatenate([left[index] for index in indices], axis=1),
            jnp.concatenate([right[index] for index in indices], axis=0),
        )

    prepare(chan, staged)
    waiting = [chan]
    for steps in WAITS:
        for step in steps:
            arrivals[step].wait_recv()
        for step in steps:
            along_y, along_z = OFFSETS[step]
            index = at_offset((along_y, RING - along_z))
            prepare(index, blocks)
            waiting.append(index)
        if steps == WAITS[1]:
            square[...] = paired(waiting)
            waiting = []
        elif ALL and steps == WAITS[2]:
            square[...] += paired(waiting)
            waiting = []

    placing.wait()
    at_place = []
    for place in range(CHAN):
        block = jnp.int32(0)
        for index in range(CHAN):
            block = jnp.where(places[index] == place, index, block)
        at_place.append(block)

    wrapped = iota((BLOCK, BLOCK), 0) > iota((BLOCK, BLOCK), 1)

    def lag_terms(delta):
        if delta == 0:
            panels = square[...] + paired(waiting)
        else:
            panels = dot(
                jnp.concatenate([left[at_place[place]] for place in range(CHAN - delta)], axis=1),
                jnp.concatenate([right[at_place[place]] for place in range(delta, CHAN)], axis=0),
            )
        sums = []
        for bin_index in range(BINS):
            for part in range(2):
                panel = panels[
                    bin_index * BLOCK : (bin_index + 1) * BLOCK, part * BLOCK : (part + 1) * BLOCK
                ]
                skewed = pltpu.roll(panel, 0, 1, stride=1, stride_axis=0)
                lags = [jnp.sum(jnp.where(wrapped, skewed, 0.0), axis=0, keepdims=True)]
                if delta > 0:
                    lags.append(jnp.sum(jnp.where(wrapped, 0.0, skewed), axis=0, keepdims=True))
                sums.append(jnp.concatenate(lags, axis=1))
        at = pl.ds(delta * SLABS, SLABS)
        for bin_index in range(BINS):
            real, imag = sums[2 * bin_index], sums[2 * bin_index + 1]
            width = real.shape[1]
            by_cos = weight_cos[bin_index, at, pl.ds(0, width)]
            by_sin = weight_sin[bin_index, at, pl.ds(0, width)]
            turned[bin_index, at, pl.ds(0, width)] = real * by_cos - imag * by_sin
            turned[bin_index, at, pl.ds(2 * BLOCK, width)] = real * by_sin + imag * by_cos

    def slant_terms(deltas):
        rows = [pl.ds(delta * SLABS, SLABS) for delta in deltas]
        width = BLOCK if deltas == (0,) else 2 * BLOCK
        lags = (pl.ds(0, width), pl.ds(2 * BLOCK, width))
        by_bin = [
            product(
                jnp.concatenate(
                    [jnp.concatenate([turned[bin_index, at, part] for at in rows], axis=0) for part in lags],
                    axis=1,
                ),
                jnp.concatenate([lag_high[bin_index, part, :] for part in lags], axis=0),
                jnp.concatenate([lag_low[bin_index, part, :] for part in lags], axis=0),
            )
            for bin_index in range(BINS)
        ]
        first = iota(by_bin[0].shape, 1) < BLOCK // 2
        plain = jnp.where(first, by_bin[0], by_bin[1])
        swapped = pltpu.roll(jnp.where(first, by_bin[1], by_bin[0]), BLOCK // 2, 1)
        for index, at in enumerate(rows):
            part = slice(index * SLABS, (index + 1) * SLABS)
            slants = plain[part] * offset_cos[at, :] + swapped[part] * offset_sin[at, :]
            terms[at] = slants.reshape(SLABS, 1, BLOCK)

    source = freq * CHAN + chan
    to_chip = {
        (flip, step): RING * lax.rem(across + flip, 2) + lax.rem(over + step, RING)
        for flip in range(2)
        for step in range(RING)
    }
    to_freq = {
        chip + (turn,): 2 * place + lax.rem(core + turn, 2)
        for chip, place in to_chip.items()
        for turn in range(2)
    }

    def post(delta, chip, turn):
        pltpu.make_async_remote_copy(
            src_ref=terms.at[delta * SLABS + to_chip[chip]],
            dst_ref=received.at[source],
            send_sem=send_term,
            recv_sem=recv_term,
            device_id={"chan": delta, "freq": to_freq[chip + (turn,)]},
            device_id_type=pl.DeviceIdType.MESH,
        ).start()

    def post_all(delta):
        for chip, turn in FAR_FIRST:
            post(delta, chip, turn)

        @pl.when(chan != delta)
        def _():
            post(delta, (0, 0), 0)

    for deltas in DELTAS:
        for delta in deltas:
            lag_terms(delta)
        slant_terms(deltas)
        if deltas == DELTAS[0]:
            pl.semaphore_wait(told_along, 3)
        for delta in deltas:
            post_all(delta)

    others = CHAN * FREQ - 1
    received[source] = terms[lax.div(chan * FREQ + freq, 2)]
    everything = received.at[pl.ds(0, others)]
    pltpu.make_async_copy(everything, everything, recv_term).wait()

    flipped[...] = received[...].reshape(FREQ * CHAN, BLOCK).T
    half_wide = WIDE // 2
    start = pl.multiple_of(lax.rem(freq, 2) * half_wide, half_wide)
    spectrum = jnp.concatenate(
        [flipped[pl.ds(start + WIDE * index, half_wide), :] for index in range(2 * BINS)],
        axis=1,
    )
    out_ref[...] = product(spectrum, time_high[...], time_low[...])

    for copy in arrivals:
        copy.wait_send()
    pltpu.make_async_copy(everything, everything, send_term).wait()


def shards(spectra, block_position):
    pairs = spectra.shape[2] // BINS
    view = spectra.reshape(2 * SEGMENTS, pairs, BINS, BLOCK)
    image = pl.pallas_call(
        kernel,
        out_shape=pltpu.VMEM((SLOWNESS // FREQ, LAG_TIMES), jnp.float32),
        in_specs=[
            pl.BlockSpec(memory_space=pl.ANY),
            pl.BlockSpec(memory_space=pl.ANY),
        ],
        out_specs=pl.BlockSpec(memory_space=pltpu.VMEM),
        scratch_shapes=[
            pltpu.SMEM((CHAN,), jnp.int32),
            pltpu.VMEM((CHAN, 2 * SEGMENTS, BINS, BLOCK), jnp.bfloat16),
            pltpu.VMEM((CHAN, 2 * SEGMENTS, BINS, BLOCK), jnp.bfloat16),
            pltpu.VMEM((CHAN, BINS * BLOCK, ROWS), jnp.bfloat16),
            pltpu.VMEM((CHAN, ROWS, 2 * BLOCK), jnp.bfloat16),
            pltpu.VMEM((BINS, CHAN * SLABS, 2 * BLOCK), jnp.float32),
            pltpu.VMEM((BINS, CHAN * SLABS, 2 * BLOCK), jnp.float32),
            pltpu.VMEM((BINS, 4 * BLOCK, BLOCK), jnp.bfloat16),
            pltpu.VMEM((BINS, 4 * BLOCK, BLOCK), jnp.bfloat16),
            pltpu.VMEM((2 * FREQS, LAG_TIMES), jnp.bfloat16),
            pltpu.VMEM((2 * FREQS, LAG_TIMES), jnp.bfloat16),
            pltpu.VMEM((CHAN * SLABS, BLOCK), jnp.float32),
            pltpu.VMEM((CHAN * SLABS, BLOCK), jnp.float32),
            pltpu.VMEM((BINS * BLOCK, 2 * BLOCK), jnp.float32),
            pltpu.VMEM((BINS, CHAN * SLABS, 4 * BLOCK), jnp.float32),
            pltpu.VMEM((CHAN * SLABS, 1, BLOCK), jnp.float32),
            pltpu.VMEM((FREQ * CHAN, 1, BLOCK), jnp.float32),
            pltpu.VMEM((BLOCK, FREQ * CHAN), jnp.float32),
            pltpu.SemaphoreType.REGULAR,
            pltpu.SemaphoreType.REGULAR,
            pltpu.SemaphoreType.DMA,
            pltpu.SemaphoreType.DMA((CHAN,)),
            pltpu.SemaphoreType.DMA((CHAN,)),
            pltpu.SemaphoreType.DMA((CHAN,)),
            pltpu.SemaphoreType.DMA,
            pltpu.SemaphoreType.DMA,
        ],
        compiler_params=pltpu.CompilerParams(collective_id=0, has_side_effects=True),
        name="slant_stack",
    )(block_position, view)
    return image.reshape(1, image.shape[0], image.shape[1])


def solution(mesh):
    return jax.shard_map(
        shards,
        mesh=mesh,
        in_specs=(P(None, None, "freq", "chan"), P()),
        out_specs=P("chan", "freq", None),
        check_vma=False,
    )
```

```python
import itertools
import math

import jax
import jax.numpy as jnp
from jax import lax
from jax.experimental import pallas as pl
from jax.experimental.pallas import tpu as pltpu
from jax.sharding import PartitionSpec as P

SEGMENTS = 32
FREQS = 256
BLOCK = 128
SLOWNESS = 256
LAG_TIMES = 512
CHAN = 8
FREQ = 16
BINS = 2
ROWS = 2 * SEGMENTS * BINS
TURN = 8 * FREQS * BLOCK
QUARTER = TURN // 4
WIDE = 32
SLABS = SLOWNESS // WIDE
RING = 4
OFFSETS = ((1, 0), (0, 1), (0, 3), (1, 1), (1, 3), (0, 2), (1, 2))
WAITS = ((0, 1), (2, 3), (4, 5), (6,))
ALL = True
DELTAS = ((0,), (1, 4, 5), (2, 3, 6, 7))
SINE = [(-1) ** k * (2 * math.pi) ** (2 * k + 1) / math.factorial(2 * k + 1) for k in range(7)]


FAR_FIRST = sorted(
    (
        (chip, turn)
        for chip in itertools.product(range(2), range(RING))
        for turn in range(2)
        if (chip, turn) != ((0, 0), 0)
    ),
    key=lambda other: -other[0][0] - min(other[0][1], RING - other[0][1]),
)


def iota(shape, axis):
    return lax.broadcasted_iota(jnp.int32, shape, axis)


def cosine(steps):
    centered = (steps & (TURN - 1)) - TURN // 2
    turn = jnp.abs(centered).astype(jnp.float32) * (1.0 / TURN) - 0.25
    square = turn * turn
    value = SINE[-1]
    for coefficient in SINE[-2::-1]:
        value = value * square + coefficient
    return value * turn


def lag_at(place):
    return jnp.where(place < BLOCK, place + 1, place - 2 * BLOCK + 1)


def split(value):
    high = value.astype(jnp.bfloat16)
    low = (value - high.astype(jnp.float32)).astype(jnp.bfloat16)
    return high, low


def dot(left, right):
    return jnp.dot(left, right, preferred_element_type=jnp.float32)


def product(left, high, low):
    rows = left.shape[0]
    left_high, left_low = split(left)
    both = dot(jnp.concatenate([left_high, left_low], axis=0), high)
    return both[:rows] + both[rows:] + dot(left_high, low)


def kernel(
    position_ref,
    spectra_ref,
    out_ref,
    places,
    staged,
    blocks,
    left,
    right,
    weight_cos,
    weight_sin,
    lag_high,
    lag_low,
    time_high,
    time_low,
    offset_cos,
    offset_sin,
    square,
    turned,
    terms,
    received,
    flipped,
    told_nearby,
    told_along,
    place_sem,
    stage_sem,
    send_block,
    recv_block,
    send_term,
    recv_term,
):
    chan = lax.axis_index("chan")
    freq = lax.axis_index("freq")

    ring, spot = chan >> 2, chan & 3

    def at_offset(offset):
        return RING * ((ring + offset[0]) & 1) + ((spot + offset[1]) & 3)

    def signal(semaphore, **target):
        pl.semaphore_signal(
            semaphore, inc=1, device_id=target, device_id_type=pl.DeviceIdType.MESH
        )

    core, over, across = freq & 1, (freq >> 1) & 3, freq >> 3
    facing = at_offset((1, 0))
    opposite = (freq + FREQ // 2) & (FREQ - 1)
    nearby = (
        {"freq": freq + 1 - 2 * core},
        {"chan": facing, "freq": opposite},
        {"chan": facing, "freq": opposite + 1 - 2 * core},
    )
    along = tuple(
        {"freq": 8 * across + 2 * ((over + step) & 3) + core} for step in (2, 1, 3)
    )

    barrier = pltpu.get_barrier_semaphore()
    for offset in OFFSETS[::-1]:
        signal(barrier, chan=at_offset(offset))
    for other in along + nearby:
        signal(barrier, **other)
    staging = [
        pltpu.make_async_copy(spectra_ref.at[:, index], staged.at[index], stage_sem.at[index])
        for index in range(CHAN)
    ]
    for copy in staging:
        copy.start()
    placing = pltpu.make_async_copy(position_ref, places, place_sem)
    placing.start()
    pl.semaphore_wait(barrier, len(OFFSETS) + 6)

    for copy in staging:
        copy.wait()
    arrivals = []
    for offset in OFFSETS:
        step, peer = len(arrivals), at_offset(offset)
        copy = pltpu.make_async_remote_copy(
            src_ref=staged.at[peer],
            dst_ref=blocks.at[chan],
            send_sem=send_block.at[step],
            recv_sem=recv_block.at[step],
            device_id={"chan": peer},
            device_id_type=pl.DeviceIdType.MESH,
        )
        copy.start()
        arrivals.append(copy)

    for other in nearby:
        signal(told_nearby, **other)

    base_bin = 2 * CHAN * freq + 2 * chan

    row = iota((CHAN * SLABS, 2 * BLOCK), 0)
    lane = iota((CHAN * SLABS, 2 * BLOCK), 1)
    offset_bin = row // SLABS
    slow = WIDE * (row % SLABS) - SLOWNESS // 2
    lag = lag_at(lane)
    count = SEGMENTS * (CHAN - offset_bin) * (BLOCK - jnp.abs(lag))
    usable = (jnp.abs(lag) < BLOCK) & ((offset_bin >= 1) | (lag >= 1))
    inverse = jnp.where(usable, 1.0 / jnp.maximum(count, 1).astype(jnp.float32), 0.0)
    for bin_index in range(BINS):
        steps = (base_bin + bin_index) * slow * (BLOCK * offset_bin + lag)
        weight_cos[bin_index] = cosine(steps) * inverse
        weight_sin[bin_index] = cosine(steps - QUARTER) * inverse

    row = iota((CHAN * SLABS, BLOCK), 0)
    lane = iota((CHAN * SLABS, BLOCK), 1)
    steps = (base_bin + lane // (2 * WIDE)) * (lane % WIDE) * (BLOCK * (row // SLABS))
    offset_cos[...] = cosine(steps)
    offset_sin[...] = cosine(steps - QUARTER)

    row = iota((2 * BLOCK, BLOCK), 0)
    lane = iota((2 * BLOCK, BLOCK), 1)
    slow = lane % WIDE
    part = (lane // WIDE) % 2
    for bin_index in range(BINS):
        swapped = (lane < BLOCK // 2) == (bin_index == 1)
        quarter = jnp.where(swapped, 1 - part, -part)
        steps = (base_bin + bin_index) * slow * lag_at(row) + QUARTER * quarter
        for row_part in range(2):
            high, low = split(cosine(steps + QUARTER * row_part))
            at = pl.ds(row_part * 2 * BLOCK, 2 * BLOCK)
            lag_high[bin_index, at, :] = high
            lag_low[bin_index, at, :] = low

    pl.semaphore_wait(told_nearby, 3)
    for other in along:
        signal(told_along, **other)

    scale = math.sqrt(SEGMENTS / FREQS)
    for bin_index in range(BINS):
        for part in range(2):
            row = iota((CHAN * FREQ, LAG_TIMES), 0)
            time = iota((CHAN * FREQ, LAG_TIMES), 1) - LAG_TIMES // 2
            steps = (2 * row + bin_index) * time * (4 * BLOCK)
            high, low = split(cosine(steps + QUARTER * part) * scale)
            at = pl.ds((2 * bin_index + part) * CHAN * FREQ, CHAN * FREQ)
            time_high[at, :] = high
            time_low[at, :] = low

    placing.wait()
    at_place = []
    for place in range(CHAN):
        block = jnp.int32(0)
        for index in range(CHAN):
            block = jnp.where(places[index] == place, index, block)
        at_place.append(block)

    odd = iota((BLOCK, ROWS), 1) % 2
    mirror = iota((BLOCK, BLOCK), 0) + iota((BLOCK, BLOCK), 1) == BLOCK - 1
    mirror = jnp.where(mirror, 1.0, 0.0).astype(jnp.bfloat16)
    half = ROWS // 2

    def prepare(index, source):
        value = source[index].reshape(ROWS, BLOCK)
        right[index, :, pl.ds(0, BLOCK)] = value
        right[index, pl.ds(0, half), pl.ds(BLOCK, BLOCK)] = value[half:]
        right[index, pl.ds(half, half), pl.ds(BLOCK, BLOCK)] = -value[:half]
        across = lax.dot_general(
            mirror, value, (((1,), (1,)), ((), ())), preferred_element_type=jnp.float32
        )
        for bin_index in range(BINS):
            left[index, pl.ds(bin_index * BLOCK, BLOCK), :] = jnp.where(
                odd == bin_index, across, 0.0
            ).astype(jnp.bfloat16)

    def paired(indices):
        return dot(
            jnp.concatenate([left[index] for index in indices], axis=1),
            jnp.concatenate([right[index] for index in indices], axis=0),
        )

    prepare(chan, staged)
    waiting = [chan]
    for steps in WAITS:
        if steps == WAITS[-1]:
            pl.semaphore_wait(told_along, 3)
        for step in steps:
            arrivals[step].wait_recv()
        for step in steps:
            along_y, along_z = OFFSETS[step]
            index = at_offset((along_y, RING - along_z))
            prepare(index, blocks)
            waiting.append(index)
        if steps == WAITS[1]:
            square[...] = paired(waiting)
            waiting = []
        elif ALL and steps == WAITS[2]:
            square[...] += paired(waiting)
            waiting = []

    wrapped = iota((BLOCK, BLOCK), 0) > iota((BLOCK, BLOCK), 1)

    def lag_terms(delta):
        if delta == 0:
            panels = square[...] + paired(waiting)
        else:
            panels = dot(
                jnp.concatenate([left[at_place[place]] for place in range(CHAN - delta)], axis=1),
                jnp.concatenate([right[at_place[place]] for place in range(delta, CHAN)], axis=0),
            )
        sums = []
        for bin_index in range(BINS):
            for part in range(2):
                panel = panels[
                    bin_index * BLOCK : (bin_index + 1) * BLOCK, part * BLOCK : (part + 1) * BLOCK
                ]
                skewed = pltpu.roll(panel, 0, 1, stride=1, stride_axis=0)
                lags = [jnp.sum(jnp.where(wrapped, skewed, 0.0), axis=0, keepdims=True)]
                if delta > 0:
                    lags.append(jnp.sum(jnp.where(wrapped, 0.0, skewed), axis=0, keepdims=True))
                sums.append(jnp.concatenate(lags, axis=1))
        at = pl.ds(delta * SLABS, SLABS)
        for bin_index in range(BINS):
            real, imag = sums[2 * bin_index], sums[2 * bin_index + 1]
            width = real.shape[1]
            by_cos = weight_cos[bin_index, at, pl.ds(0, width)]
            by_sin = weight_sin[bin_index, at, pl.ds(0, width)]
            turned[bin_index, at, pl.ds(0, width)] = real * by_cos - imag * by_sin
            turned[bin_index, at, pl.ds(2 * BLOCK, width)] = real * by_sin + imag * by_cos

    def slant_terms(deltas):
        rows = [pl.ds(delta * SLABS, SLABS) for delta in deltas]
        width = BLOCK if deltas == (0,) else 2 * BLOCK
        lags = (pl.ds(0, width), pl.ds(2 * BLOCK, width))
        by_bin = [
            product(
                jnp.concatenate(
                    [jnp.concatenate([turned[bin_index, at, part] for at in rows], axis=0) for part in lags],
                    axis=1,
                ),
                jnp.concatenate([lag_high[bin_index, part, :] for part in lags], axis=0),
                jnp.concatenate([lag_low[bin_index, part, :] for part in lags], axis=0),
            )
            for bin_index in range(BINS)
        ]
        first = iota(by_bin[0].shape, 1) < BLOCK // 2
        plain = jnp.where(first, by_bin[0], by_bin[1])
        swapped = pltpu.roll(jnp.where(first, by_bin[1], by_bin[0]), BLOCK // 2, 1)
        for index, at in enumerate(rows):
            part = slice(index * SLABS, (index + 1) * SLABS)
            slants = plain[part] * offset_cos[at, :] + swapped[part] * offset_sin[at, :]
            terms[at] = slants.reshape(SLABS, 1, BLOCK)

    source = freq * CHAN + chan
    to_chip = {
        (flip, step): RING * ((across + flip) & 1) + ((over + step) & 3)
        for flip in range(2)
        for step in range(RING)
    }
    to_freq = {
        chip + (turn,): 2 * place + ((core + turn) & 1)
        for chip, place in to_chip.items()
        for turn in range(2)
    }

    def post(delta, chip, turn):
        pltpu.make_async_remote_copy(
            src_ref=terms.at[delta * SLABS + to_chip[chip]],
            dst_ref=received.at[source],
            send_sem=send_term,
            recv_sem=recv_term,
            device_id={"chan": delta, "freq": to_freq[chip + (turn,)]},
            device_id_type=pl.DeviceIdType.MESH,
        ).start()

    def post_all(delta):
        for chip, turn in FAR_FIRST:
            post(delta, chip, turn)

        @pl.when(chan != delta)
        def _():
            post(delta, (0, 0), 0)

    for deltas in DELTAS:
        for delta in deltas:
            lag_terms(delta)
        slant_terms(deltas)
        for delta in deltas:
            post_all(delta)

    others = CHAN * FREQ - 1
    received[source] = terms[(chan * FREQ + freq) >> 1]
    everything = received.at[pl.ds(0, others)]
    for copy in arrivals:
        copy.wait_send()
    pltpu.make_async_copy(everything, everything, send_term).wait()
    pltpu.make_async_copy(everything, everything, recv_term).wait()

    flipped[...] = received[...].reshape(FREQ * CHAN, BLOCK).T
    half_wide = WIDE // 2
    start = pl.multiple_of(core * half_wide, half_wide)
    spectrum = jnp.concatenate(
        [flipped[pl.ds(start + WIDE * index, half_wide), :] for index in range(2 * BINS)],
        axis=1,
    )
    out_ref[...] = product(spectrum, time_high[...], time_low[...])


def shards(spectra, block_position):
    pairs = spectra.shape[2] // BINS
    view = spectra.reshape(2 * SEGMENTS, pairs, BINS, BLOCK)
    image = pl.pallas_call(
        kernel,
        out_shape=pltpu.VMEM((SLOWNESS // FREQ, LAG_TIMES), jnp.float32),
        in_specs=[
            pl.BlockSpec(memory_space=pl.ANY),
            pl.BlockSpec(memory_space=pl.ANY),
        ],
        out_specs=pl.BlockSpec(memory_space=pltpu.VMEM),
        scratch_shapes=[
            pltpu.SMEM((CHAN,), jnp.int32),
            pltpu.VMEM((CHAN, 2 * SEGMENTS, BINS, BLOCK), jnp.bfloat16),
            pltpu.VMEM((CHAN, 2 * SEGMENTS, BINS, BLOCK), jnp.bfloat16),
            pltpu.VMEM((CHAN, BINS * BLOCK, ROWS), jnp.bfloat16),
            pltpu.VMEM((CHAN, ROWS, 2 * BLOCK), jnp.bfloat16),
            pltpu.VMEM((BINS, CHAN * SLABS, 2 * BLOCK), jnp.float32),
            pltpu.VMEM((BINS, CHAN * SLABS, 2 * BLOCK), jnp.float32),
            pltpu.VMEM((BINS, 4 * BLOCK, BLOCK), jnp.bfloat16),
            pltpu.VMEM((BINS, 4 * BLOCK, BLOCK), jnp.bfloat16),
            pltpu.VMEM((2 * FREQS, LAG_TIMES), jnp.bfloat16),
            pltpu.VMEM((2 * FREQS, LAG_TIMES), jnp.bfloat16),
            pltpu.VMEM((CHAN * SLABS, BLOCK), jnp.float32),
            pltpu.VMEM((CHAN * SLABS, BLOCK), jnp.float32),
            pltpu.VMEM((BINS * BLOCK, 2 * BLOCK), jnp.float32),
            pltpu.VMEM((BINS, CHAN * SLABS, 4 * BLOCK), jnp.float32),
            pltpu.VMEM((CHAN * SLABS, 1, BLOCK), jnp.float32),
            pltpu.VMEM((FREQ * CHAN, 1, BLOCK), jnp.float32),
            pltpu.VMEM((BLOCK, FREQ * CHAN), jnp.float32),
            pltpu.SemaphoreType.REGULAR,
            pltpu.SemaphoreType.REGULAR,
            pltpu.SemaphoreType.DMA,
            pltpu.SemaphoreType.DMA((CHAN,)),
            pltpu.SemaphoreType.DMA((CHAN,)),
            pltpu.SemaphoreType.DMA((CHAN,)),
            pltpu.SemaphoreType.DMA,
            pltpu.SemaphoreType.DMA,
        ],
        compiler_params=pltpu.CompilerParams(collective_id=0, has_side_effects=True),
        name="slant_stack",
    )(block_position, view)
    return image.reshape(1, image.shape[0], image.shape[1])


def solution(mesh):
    return jax.shard_map(
        shards,
        mesh=mesh,
        in_specs=(P(None, None, "freq", "chan"), P()),
        out_specs=P("chan", "freq", None),
        check_vma=False,
    )
```

```python
import itertools
import math

import jax
import jax.numpy as jnp
from jax import lax
from jax.experimental import pallas as pl
from jax.experimental.pallas import tpu as pltpu
from jax.sharding import PartitionSpec as P

SEGMENTS = 32
FREQS = 256
BLOCK = 128
SLOWNESS = 256
LAG_TIMES = 512
CHAN = 8
FREQ = 16
BINS = 2
ROWS = 2 * SEGMENTS * BINS
TURN = 8 * FREQS * BLOCK
QUARTER = TURN // 4
WIDE = 32
SLABS = SLOWNESS // WIDE
RING = 4
OFFSETS = ((1, 0), (0, 1), (0, 3), (1, 1), (1, 3), (0, 2), (1, 2))
WAITS = ((0, 1), (2, 3), (4, 5), (6,))
ALL = True
DELTAS = ((0,), (1, 4, 5), (2, 3, 6, 7))
SINE = [(-1) ** k * (2 * math.pi) ** (2 * k + 1) / math.factorial(2 * k + 1) for k in range(7)]


FAR_FIRST = sorted(
    (
        (chip, turn)
        for chip in itertools.product(range(2), range(RING))
        for turn in range(2)
        if (chip, turn) != ((0, 0), 0)
    ),
    key=lambda other: -other[0][0] - min(other[0][1], RING - other[0][1]),
)


def iota(shape, axis):
    return lax.broadcasted_iota(jnp.int32, shape, axis)


def cosine(steps):
    centered = (steps & (TURN - 1)) - TURN // 2
    turn = jnp.abs(centered).astype(jnp.float32) * (1.0 / TURN) - 0.25
    square = turn * turn
    value = SINE[-1]
    for coefficient in SINE[-2::-1]:
        value = value * square + coefficient
    return value * turn


def lag_at(place):
    return jnp.where(place < BLOCK, place + 1, place - 2 * BLOCK + 1)


def split(value):
    high = value.astype(jnp.bfloat16)
    low = (value - high.astype(jnp.float32)).astype(jnp.bfloat16)
    return high, low


def dot(left, right):
    return jnp.dot(left, right, preferred_element_type=jnp.float32)


def product(left, high, low):
    rows = left.shape[0]
    left_high, left_low = split(left)
    both = dot(jnp.concatenate([left_high, left_low], axis=0), high)
    return both[:rows] + both[rows:] + dot(left_high, low)


def kernel(
    position_ref,
    spectra_ref,
    out_ref,
    places,
    staged,
    blocks,
    left,
    right,
    weight_cos,
    weight_sin,
    lag_high,
    lag_low,
    time_high,
    time_low,
    offset_cos,
    offset_sin,
    square,
    turned,
    terms,
    received,
    told_nearby,
    told_along,
    place_sem,
    stage_sem,
    send_block,
    recv_block,
    send_term,
    recv_term,
):
    chan = lax.axis_index("chan")
    freq = lax.axis_index("freq")

    ring, spot = chan >> 2, chan & 3

    def at_offset(offset):
        return RING * ((ring + offset[0]) & 1) + ((spot + offset[1]) & 3)

    def signal(semaphore, **target):
        pl.semaphore_signal(
            semaphore, inc=1, device_id=target, device_id_type=pl.DeviceIdType.MESH
        )

    core, over, across = freq & 1, (freq >> 1) & 3, freq >> 3
    facing = at_offset((1, 0))
    opposite = (freq + FREQ // 2) & (FREQ - 1)
    nearby = (
        {"freq": freq + 1 - 2 * core},
        {"chan": facing, "freq": opposite},
        {"chan": facing, "freq": opposite + 1 - 2 * core},
    )
    along = tuple(
        {"freq": 8 * across + 2 * ((over + step) & 3) + core} for step in (2, 1, 3)
    )

    barrier = pltpu.get_barrier_semaphore()
    for offset in OFFSETS[::-1]:
        signal(barrier, chan=at_offset(offset))
    for other in along + nearby:
        signal(barrier, **other)
    staging = [
        pltpu.make_async_copy(spectra_ref.at[:, index], staged.at[index], stage_sem.at[index])
        for index in range(CHAN)
    ]
    for copy in staging:
        copy.start()
    placing = pltpu.make_async_copy(position_ref, places, place_sem)
    placing.start()
    pl.semaphore_wait(barrier, len(OFFSETS) + 6)

    for copy in staging:
        copy.wait()
    arrivals = []
    for offset in OFFSETS:
        step, peer = len(arrivals), at_offset(offset)
        copy = pltpu.make_async_remote_copy(
            src_ref=staged.at[peer],
            dst_ref=blocks.at[chan],
            send_sem=send_block.at[step],
            recv_sem=recv_block.at[step],
            device_id={"chan": peer},
            device_id_type=pl.DeviceIdType.MESH,
        )
        copy.start()
        arrivals.append(copy)

    for other in nearby:
        signal(told_nearby, **other)

    base_bin = 2 * CHAN * freq + 2 * chan

    row = iota((CHAN * SLABS, 2 * BLOCK), 0)
    lane = iota((CHAN * SLABS, 2 * BLOCK), 1)
    offset_bin = row // SLABS
    slow = WIDE * (row % SLABS) - SLOWNESS // 2
    lag = lag_at(lane)
    count = SEGMENTS * (CHAN - offset_bin) * (BLOCK - jnp.abs(lag))
    usable = (jnp.abs(lag) < BLOCK) & ((offset_bin >= 1) | (lag >= 1))
    inverse = jnp.where(usable, 1.0 / jnp.maximum(count, 1).astype(jnp.float32), 0.0)
    for bin_index in range(BINS):
        steps = (base_bin + bin_index) * slow * (BLOCK * offset_bin + lag)
        weight_cos[bin_index] = cosine(steps) * inverse
        weight_sin[bin_index] = cosine(steps - QUARTER) * inverse

    row = iota((CHAN * SLABS, BLOCK), 0)
    lane = iota((CHAN * SLABS, BLOCK), 1)
    steps = (base_bin + lane // (2 * WIDE)) * (lane % WIDE) * (BLOCK * (row // SLABS))
    offset_cos[...] = cosine(steps)
    offset_sin[...] = cosine(steps - QUARTER)

    row = iota((2 * BLOCK, BLOCK), 0)
    lane = iota((2 * BLOCK, BLOCK), 1)
    slow = lane % WIDE
    part = (lane // WIDE) % 2
    for bin_index in range(BINS):
        swapped = (lane < BLOCK // 2) == (bin_index == 1)
        quarter = jnp.where(swapped, 1 - part, -part)
        steps = (base_bin + bin_index) * slow * lag_at(row) + QUARTER * quarter
        for row_part in range(2):
            high, low = split(cosine(steps + QUARTER * row_part))
            at = pl.ds(row_part * 2 * BLOCK, 2 * BLOCK)
            lag_high[bin_index, at, :] = high
            lag_low[bin_index, at, :] = low

    pl.semaphore_wait(told_nearby, 3)
    for other in along:
        signal(told_along, **other)

    scale = math.sqrt(SEGMENTS / FREQS)
    for bin_index in range(BINS):
        for part in range(2):
            row = iota((CHAN * FREQ, LAG_TIMES), 0)
            time = iota((CHAN * FREQ, LAG_TIMES), 1) - LAG_TIMES // 2
            steps = (2 * row + bin_index) * time * (4 * BLOCK)
            high, low = split(cosine(steps + QUARTER * part) * scale)
            at = pl.ds((2 * bin_index + part) * CHAN * FREQ, CHAN * FREQ)
            time_high[at, :] = high
            time_low[at, :] = low

    placing.wait()
    at_place = []
    for place in range(CHAN):
        block = jnp.int32(0)
        for index in range(CHAN):
            block = jnp.where(places[index] == place, index, block)
        at_place.append(block)

    odd = iota((BLOCK, ROWS), 1) % 2
    mirror = iota((BLOCK, BLOCK), 0) + iota((BLOCK, BLOCK), 1) == BLOCK - 1
    mirror = jnp.where(mirror, 1.0, 0.0).astype(jnp.bfloat16)
    half = ROWS // 2

    def prepare(index, source):
        value = source[index].reshape(ROWS, BLOCK)
        swapped = jnp.concatenate([value[half:], -value[:half]], axis=0)
        both = jnp.concatenate([value, swapped], axis=1)
        across = lax.dot_general(
            mirror, value, (((1,), (1,)), ((), ())), preferred_element_type=jnp.float32
        )
        masked = jnp.concatenate(
            [jnp.where(odd == bin_index, across, 0.0) for bin_index in range(BINS)], axis=0
        ).astype(jnp.bfloat16)
        right[index] = both
        left[index] = masked
        return masked, both

    def paired(indices):
        return dot(
            jnp.concatenate([left[index] for index in indices], axis=1),
            jnp.concatenate([right[index] for index in indices], axis=0),
        )

    prepare(chan, staged)
    waiting = [chan]
    for steps in WAITS:
        if steps == WAITS[-1]:
            pl.semaphore_wait(told_along, 3)
        for step in steps:
            arrivals[step].wait_recv()
        for step in steps:
            along_y, along_z = OFFSETS[step]
            index = at_offset((along_y, RING - along_z))
            newest = prepare(index, blocks)
            waiting.append(index)
        if steps == WAITS[1]:
            square[...] = paired(waiting)
            waiting = []
        elif ALL and steps == WAITS[2]:
            square[...] += paired(waiting)
            waiting = []

    wrapped = iota((BLOCK, BLOCK), 0) > iota((BLOCK, BLOCK), 1)

    def lag_terms(delta):
        if delta == 0:
            panels = square[...] + dot(*newest)
        else:
            panels = dot(
                jnp.concatenate([left[at_place[place]] for place in range(CHAN - delta)], axis=1),
                jnp.concatenate([right[at_place[place]] for place in range(delta, CHAN)], axis=0),
            )
        sums = []
        for bin_index in range(BINS):
            for part in range(2):
                panel = panels[
                    bin_index * BLOCK : (bin_index + 1) * BLOCK, part * BLOCK : (part + 1) * BLOCK
                ]
                skewed = pltpu.roll(panel, 0, 1, stride=1, stride_axis=0)
                lags = [jnp.sum(jnp.where(wrapped, skewed, 0.0), axis=0, keepdims=True)]
                if delta > 0:
                    lags.append(jnp.sum(jnp.where(wrapped, 0.0, skewed), axis=0, keepdims=True))
                sums.append(jnp.concatenate(lags, axis=1))
        at = pl.ds(delta * SLABS, SLABS)
        for bin_index in range(BINS):
            real, imag = sums[2 * bin_index], sums[2 * bin_index + 1]
            width = real.shape[1]
            by_cos = weight_cos[bin_index, at, pl.ds(0, width)]
            by_sin = weight_sin[bin_index, at, pl.ds(0, width)]
            turned[bin_index, at, pl.ds(0, width)] = real * by_cos - imag * by_sin
            turned[bin_index, at, pl.ds(2 * BLOCK, width)] = real * by_sin + imag * by_cos

    def slant_terms(deltas):
        rows = [pl.ds(delta * SLABS, SLABS) for delta in deltas]
        width = BLOCK if deltas == (0,) else 2 * BLOCK
        lags = (pl.ds(0, width), pl.ds(2 * BLOCK, width))
        by_bin = [
            product(
                jnp.concatenate(
                    [jnp.concatenate([turned[bin_index, at, part] for at in rows], axis=0) for part in lags],
                    axis=1,
                ),
                jnp.concatenate([lag_high[bin_index, part, :] for part in lags], axis=0),
                jnp.concatenate([lag_low[bin_index, part, :] for part in lags], axis=0),
            )
            for bin_index in range(BINS)
        ]
        first = iota(by_bin[0].shape, 1) < BLOCK // 2
        plain = jnp.where(first, by_bin[0], by_bin[1])
        swapped = pltpu.roll(jnp.where(first, by_bin[1], by_bin[0]), BLOCK // 2, 1)
        for index, at in enumerate(rows):
            part = slice(index * SLABS, (index + 1) * SLABS)
            slants = plain[part] * offset_cos[at, :] + swapped[part] * offset_sin[at, :]
            terms[at] = slants.reshape(SLABS, 1, BLOCK)

    source = freq * CHAN + chan
    to_chip = {
        (flip, step): RING * ((across + flip) & 1) + ((over + step) & 3)
        for flip in range(2)
        for step in range(RING)
    }
    to_freq = {
        chip + (turn,): 2 * place + ((core + turn) & 1)
        for chip, place in to_chip.items()
        for turn in range(2)
    }

    def post(delta, chip, turn):
        pltpu.make_async_remote_copy(
            src_ref=terms.at[delta * SLABS + to_chip[chip]],
            dst_ref=received.at[source],
            send_sem=send_term,
            recv_sem=recv_term,
            device_id={"chan": delta, "freq": to_freq[chip + (turn,)]},
            device_id_type=pl.DeviceIdType.MESH,
        ).start()

    def post_all(delta):
        for chip, turn in FAR_FIRST:
            post(delta, chip, turn)

        @pl.when(chan != delta)
        def _():
            post(delta, (0, 0), 0)

    for deltas in DELTAS:
        for delta in deltas:
            lag_terms(delta)
        slant_terms(deltas)
        for delta in deltas:
            post_all(delta)

    others = CHAN * FREQ - 1
    received[source] = terms[(chan * FREQ + freq) >> 1]
    everything = received.at[pl.ds(0, others)]
    for copy in arrivals:
        copy.wait_send()
    pltpu.make_async_copy(everything, everything, send_term).wait()
    pltpu.make_async_copy(everything, everything, recv_term).wait()

    flipped = received[...].reshape(FREQ * CHAN, BLOCK).T
    half_wide = WIDE // 2
    halves = [
        jnp.concatenate(
            [flipped[start + WIDE * index : start + WIDE * index + half_wide] for index in range(2 * BINS)],
            axis=1,
        )
        for start in (0, half_wide)
    ]
    spectrum = jnp.where(core == 0, halves[0], halves[1])
    out_ref[...] = product(spectrum, time_high[...], time_low[...])


def shards(spectra, block_position):
    pairs = spectra.shape[2] // BINS
    view = spectra.reshape(2 * SEGMENTS, pairs, BINS, BLOCK)
    image = pl.pallas_call(
        kernel,
        out_shape=pltpu.VMEM((SLOWNESS // FREQ, LAG_TIMES), jnp.float32),
        in_specs=[
            pl.BlockSpec(memory_space=pl.ANY),
            pl.BlockSpec(memory_space=pl.ANY),
        ],
        out_specs=pl.BlockSpec(memory_space=pltpu.VMEM),
        scratch_shapes=[
            pltpu.SMEM((CHAN,), jnp.int32),
            pltpu.VMEM((CHAN, 2 * SEGMENTS, BINS, BLOCK), jnp.bfloat16),
            pltpu.VMEM((CHAN, 2 * SEGMENTS, BINS, BLOCK), jnp.bfloat16),
            pltpu.VMEM((CHAN, BINS * BLOCK, ROWS), jnp.bfloat16),
            pltpu.VMEM((CHAN, ROWS, 2 * BLOCK), jnp.bfloat16),
            pltpu.VMEM((BINS, CHAN * SLABS, 2 * BLOCK), jnp.float32),
            pltpu.VMEM((BINS, CHAN * SLABS, 2 * BLOCK), jnp.float32),
            pltpu.VMEM((BINS, 4 * BLOCK, BLOCK), jnp.bfloat16),
            pltpu.VMEM((BINS, 4 * BLOCK, BLOCK), jnp.bfloat16),
            pltpu.VMEM((2 * FREQS, LAG_TIMES), jnp.bfloat16),
            pltpu.VMEM((2 * FREQS, LAG_TIMES), jnp.bfloat16),
            pltpu.VMEM((CHAN * SLABS, BLOCK), jnp.float32),
            pltpu.VMEM((CHAN * SLABS, BLOCK), jnp.float32),
            pltpu.VMEM((BINS * BLOCK, 2 * BLOCK), jnp.float32),
            pltpu.VMEM((BINS, CHAN * SLABS, 4 * BLOCK), jnp.float32),
            pltpu.VMEM((CHAN * SLABS, 1, BLOCK), jnp.float32),
            pltpu.VMEM((FREQ * CHAN, 1, BLOCK), jnp.float32),
            pltpu.SemaphoreType.REGULAR,
            pltpu.SemaphoreType.REGULAR,
            pltpu.SemaphoreType.DMA,
            pltpu.SemaphoreType.DMA((CHAN,)),
            pltpu.SemaphoreType.DMA((CHAN,)),
            pltpu.SemaphoreType.DMA((CHAN,)),
            pltpu.SemaphoreType.DMA,
            pltpu.SemaphoreType.DMA,
        ],
        compiler_params=pltpu.CompilerParams(collective_id=0, has_side_effects=True),
        name="slant_stack",
    )(block_position, view)
    return image.reshape(1, image.shape[0], image.shape[1])


def solution(mesh):
    return jax.shard_map(
        shards,
        mesh=mesh,
        in_specs=(P(None, None, "freq", "chan"), P()),
        out_specs=P("chan", "freq", None),
        check_vma=False,
    )
```

```python
import itertools
import math

import jax
import jax.numpy as jnp
from jax import lax
from jax.experimental import pallas as pl
from jax.experimental.pallas import tpu as pltpu
from jax.sharding import PartitionSpec as P

SEGMENTS = 32
FREQS = 256
BLOCK = 128
SLOWNESS = 256
LAG_TIMES = 512
CHAN = 8
FREQ = 16
BINS = 2
ROWS = 2 * SEGMENTS * BINS
TURN = 8 * FREQS * BLOCK
QUARTER = TURN // 4
WIDE = 32
SLABS = SLOWNESS // WIDE
RING = 4
OFFSETS = ((1, 0), (0, 1), (0, 3), (1, 1), (1, 3), (0, 2), (1, 2))
WAITS = ((0, 1), (2, 3), (4, 5), (6,))
ALL = True
DELTAS = ((0,), (1, 4), (2, 3, 5, 6, 7))
SINE = [(-1) ** k * (2 * math.pi) ** (2 * k + 1) / math.factorial(2 * k + 1) for k in range(7)]


FAR_FIRST = sorted(
    (
        (chip, turn)
        for chip in itertools.product(range(2), range(RING))
        for turn in range(2)
        if (chip, turn) != ((0, 0), 0)
    ),
    key=lambda other: -other[0][0] - min(other[0][1], RING - other[0][1]),
)


def iota(shape, axis):
    return lax.broadcasted_iota(jnp.int32, shape, axis)


def cosine(steps):
    centered = (steps & (TURN - 1)) - TURN // 2
    turn = jnp.abs(centered).astype(jnp.float32) * (1.0 / TURN) - 0.25
    square = turn * turn
    value = SINE[-1]
    for coefficient in SINE[-2::-1]:
        value = value * square + coefficient
    return value * turn


def lag_at(place):
    return jnp.where(place < BLOCK, place + 1, place - 2 * BLOCK + 1)


def split(value):
    high = value.astype(jnp.bfloat16)
    low = (value - high.astype(jnp.float32)).astype(jnp.bfloat16)
    return high, low


def dot(left, right):
    return jnp.dot(left, right, preferred_element_type=jnp.float32)


def product(left, high, low):
    rows = left.shape[0]
    left_high, left_low = split(left)
    both = dot(jnp.concatenate([left_high, left_low], axis=0), high)
    return both[:rows] + both[rows:] + dot(left_high, low)


def kernel(
    position_ref,
    spectra_ref,
    out_ref,
    places,
    staged,
    blocks,
    left,
    right,
    weight_cos,
    weight_sin,
    lag_high,
    lag_low,
    time_high,
    time_low,
    offset_cos,
    offset_sin,
    square,
    turned,
    terms,
    received,
    told_nearby,
    told_along,
    place_sem,
    stage_sem,
    send_block,
    recv_block,
    send_term,
    recv_term,
):
    chan = lax.axis_index("chan")
    freq = lax.axis_index("freq")

    ring, spot = chan >> 2, chan & 3

    def at_offset(offset):
        return RING * ((ring + offset[0]) & 1) + ((spot + offset[1]) & 3)

    def signal(semaphore, **target):
        pl.semaphore_signal(
            semaphore, inc=1, device_id=target, device_id_type=pl.DeviceIdType.MESH
        )

    core, over, across = freq & 1, (freq >> 1) & 3, freq >> 3
    facing = at_offset((1, 0))
    opposite = (freq + FREQ // 2) & (FREQ - 1)
    nearby = (
        {"freq": freq + 1 - 2 * core},
        {"chan": facing, "freq": opposite},
        {"chan": facing, "freq": opposite + 1 - 2 * core},
    )
    along = tuple(
        {"freq": 8 * across + 2 * ((over + step) & 3) + core} for step in (2, 1, 3)
    )

    barrier = pltpu.get_barrier_semaphore()
    for offset in OFFSETS[::-1]:
        signal(barrier, chan=at_offset(offset))
    for other in along + nearby:
        signal(barrier, **other)
    staging = [
        pltpu.make_async_copy(spectra_ref.at[:, index], staged.at[index], stage_sem.at[index])
        for index in range(CHAN)
    ]
    for copy in staging:
        copy.start()
    placing = pltpu.make_async_copy(position_ref, places, place_sem)
    placing.start()
    pl.semaphore_wait(barrier, len(OFFSETS) + 6)

    for copy in staging:
        copy.wait()
    arrivals = []
    for offset in OFFSETS:
        step, peer = len(arrivals), at_offset(offset)
        copy = pltpu.make_async_remote_copy(
            src_ref=staged.at[peer],
            dst_ref=blocks.at[chan],
            send_sem=send_block.at[step],
            recv_sem=recv_block.at[step],
            device_id={"chan": peer},
            device_id_type=pl.DeviceIdType.MESH,
        )
        copy.start()
        arrivals.append(copy)

    for other in nearby:
        signal(told_nearby, **other)

    base_bin = 2 * CHAN * freq + 2 * chan

    row = iota((CHAN * SLABS, 2 * BLOCK), 0)
    lane = iota((CHAN * SLABS, 2 * BLOCK), 1)
    offset_bin = row // SLABS
    slow = WIDE * (row % SLABS) - SLOWNESS // 2
    lag = lag_at(lane)
    count = SEGMENTS * (CHAN - offset_bin) * (BLOCK - jnp.abs(lag))
    usable = (jnp.abs(lag) < BLOCK) & ((offset_bin >= 1) | (lag >= 1))
    inverse = jnp.where(usable, 1.0 / jnp.maximum(count, 1).astype(jnp.float32), 0.0)
    for bin_index in range(BINS):
        steps = (base_bin + bin_index) * slow * (BLOCK * offset_bin + lag)
        weight_cos[bin_index] = cosine(steps) * inverse
        weight_sin[bin_index] = cosine(steps - QUARTER) * inverse

    row = iota((CHAN * SLABS, BLOCK), 0)
    lane = iota((CHAN * SLABS, BLOCK), 1)
    steps = (base_bin + lane // (2 * WIDE)) * (lane % WIDE) * (BLOCK * (row // SLABS))
    offset_cos[...] = cosine(steps)
    offset_sin[...] = cosine(steps - QUARTER)

    row = iota((2 * BLOCK, BLOCK), 0)
    lane = iota((2 * BLOCK, BLOCK), 1)
    slow = lane % WIDE
    part = (lane // WIDE) % 2
    for bin_index in range(BINS):
        swapped = (lane < BLOCK // 2) == (bin_index == 1)
        quarter = jnp.where(swapped, 1 - part, -part)
        steps = (base_bin + bin_index) * slow * lag_at(row) + QUARTER * quarter
        for row_part in range(2):
            high, low = split(cosine(steps + QUARTER * row_part))
            at = pl.ds(row_part * 2 * BLOCK, 2 * BLOCK)
            lag_high[bin_index, at, :] = high
            lag_low[bin_index, at, :] = low

    pl.semaphore_wait(told_nearby, 3)
    for other in along:
        signal(told_along, **other)

    scale = math.sqrt(SEGMENTS / FREQS)
    for bin_index in range(BINS):
        for part in range(2):
            row = iota((CHAN * FREQ, LAG_TIMES), 0)
            time = iota((CHAN * FREQ, LAG_TIMES), 1) - LAG_TIMES // 2
            steps = (2 * row + bin_index) * time * (4 * BLOCK)
            high, low = split(cosine(steps + QUARTER * part) * scale)
            at = pl.ds((2 * bin_index + part) * CHAN * FREQ, CHAN * FREQ)
            time_high[at, :] = high
            time_low[at, :] = low

    placing.wait()
    at_place = []
    for place in range(CHAN):
        block = jnp.int32(0)
        for index in range(CHAN):
            block = jnp.where(places[index] == place, index, block)
        at_place.append(block)

    odd = iota((BLOCK, ROWS), 1) % 2
    mirror = iota((BLOCK, BLOCK), 0) + iota((BLOCK, BLOCK), 1) == BLOCK - 1
    mirror = jnp.where(mirror, 1.0, 0.0).astype(jnp.bfloat16)
    half = ROWS // 2

    def prepare(index, source):
        value = source[index].reshape(ROWS, BLOCK)
        swapped = jnp.concatenate([value[half:], -value[:half]], axis=0)
        both = jnp.concatenate([value, swapped], axis=1)
        across = lax.dot_general(
            mirror, value, (((1,), (1,)), ((), ())), preferred_element_type=jnp.float32
        )
        masked = jnp.concatenate(
            [jnp.where(odd == bin_index, across, 0.0) for bin_index in range(BINS)], axis=0
        ).astype(jnp.bfloat16)
        right[index] = both
        left[index] = masked
        return masked, both

    def paired(indices):
        return dot(
            jnp.concatenate([left[index] for index in indices], axis=1),
            jnp.concatenate([right[index] for index in indices], axis=0),
        )

    prepare(chan, staged)
    waiting = [chan]
    for steps in WAITS:
        if steps == WAITS[-1]:
            pl.semaphore_wait(told_along, 3)
        for step in steps:
            arrivals[step].wait_recv()
        for step in steps:
            along_y, along_z = OFFSETS[step]
            index = at_offset((along_y, RING - along_z))
            newest = prepare(index, blocks)
            waiting.append(index)
        if steps == WAITS[1]:
            square[...] = paired(waiting)
            waiting = []
        elif ALL and steps == WAITS[2]:
            square[...] += paired(waiting)
            waiting = []

    wrapped = iota((BLOCK, BLOCK), 0) > iota((BLOCK, BLOCK), 1)

    def lag_terms(delta):
        if delta == 0:
            panels = square[...] + dot(*newest)
        else:
            panels = dot(
                jnp.concatenate([left[at_place[place]] for place in range(CHAN - delta)], axis=1),
                jnp.concatenate([right[at_place[place]] for place in range(delta, CHAN)], axis=0),
            )
        sums = []
        for bin_index in range(BINS):
            for part in range(2):
                panel = panels[
                    bin_index * BLOCK : (bin_index + 1) * BLOCK, part * BLOCK : (part + 1) * BLOCK
                ]
                skewed = pltpu.roll(panel, 0, 1, stride=1, stride_axis=0)
                lags = [jnp.sum(jnp.where(wrapped, skewed, 0.0), axis=0, keepdims=True)]
                if delta > 0:
                    lags.append(jnp.sum(jnp.where(wrapped, 0.0, skewed), axis=0, keepdims=True))
                sums.append(jnp.concatenate(lags, axis=1))
        at = pl.ds(delta * SLABS, SLABS)
        for bin_index in range(BINS):
            real, imag = sums[2 * bin_index], sums[2 * bin_index + 1]
            width = real.shape[1]
            by_cos = weight_cos[bin_index, at, pl.ds(0, width)]
            by_sin = weight_sin[bin_index, at, pl.ds(0, width)]
            turned[bin_index, at, pl.ds(0, width)] = real * by_cos - imag * by_sin
            turned[bin_index, at, pl.ds(2 * BLOCK, width)] = real * by_sin + imag * by_cos

    def slant_terms(deltas):
        rows = [pl.ds(delta * SLABS, SLABS) for delta in deltas]
        width = BLOCK if deltas == (0,) else 2 * BLOCK
        lags = (pl.ds(0, width), pl.ds(2 * BLOCK, width))
        by_bin = [
            product(
                jnp.concatenate(
                    [jnp.concatenate([turned[bin_index, at, part] for at in rows], axis=0) for part in lags],
                    axis=1,
                ),
                jnp.concatenate([lag_high[bin_index, part, :] for part in lags], axis=0),
                jnp.concatenate([lag_low[bin_index, part, :] for part in lags], axis=0),
            )
            for bin_index in range(BINS)
        ]
        first = iota(by_bin[0].shape, 1) < BLOCK // 2
        plain = jnp.where(first, by_bin[0], by_bin[1])
        swapped = pltpu.roll(jnp.where(first, by_bin[1], by_bin[0]), BLOCK // 2, 1)
        for index, at in enumerate(rows):
            part = slice(index * SLABS, (index + 1) * SLABS)
            slants = plain[part] * offset_cos[at, :] + swapped[part] * offset_sin[at, :]
            terms[at] = slants.reshape(SLABS, 1, BLOCK)

    source = freq * CHAN + chan
    to_chip = {
        (flip, step): RING * ((across + flip) & 1) + ((over + step) & 3)
        for flip in range(2)
        for step in range(RING)
    }
    to_freq = {
        chip + (turn,): 2 * place + ((core + turn) & 1)
        for chip, place in to_chip.items()
        for turn in range(2)
    }

    def post(delta, chip, turn):
        pltpu.make_async_remote_copy(
            src_ref=terms.at[delta * SLABS + to_chip[chip]],
            dst_ref=received.at[source],
            send_sem=send_term,
            recv_sem=recv_term,
            device_id={"chan": delta, "freq": to_freq[chip + (turn,)]},
            device_id_type=pl.DeviceIdType.MESH,
        ).start()

    def post_all(delta):
        for chip, turn in FAR_FIRST:
            post(delta, chip, turn)

        @pl.when(chan != delta)
        def _():
            post(delta, (0, 0), 0)

    for deltas in DELTAS:
        for delta in deltas:
            lag_terms(delta)
        slant_terms(deltas)
        for delta in deltas:
            post_all(delta)

    others = CHAN * FREQ - 1
    received[source] = terms[(chan * FREQ + freq) >> 1]
    everything = received.at[pl.ds(0, others)]
    for copy in arrivals:
        copy.wait_send()
    pltpu.make_async_copy(everything, everything, send_term).wait()
    pltpu.make_async_copy(everything, everything, recv_term).wait()

    flipped = received[...].reshape(FREQ * CHAN, BLOCK).T
    half_wide = WIDE // 2
    halves = [
        jnp.concatenate(
            [flipped[start + WIDE * index : start + WIDE * index + half_wide] for index in range(2 * BINS)],
            axis=1,
        )
        for start in (0, half_wide)
    ]
    spectrum = jnp.where(core == 0, halves[0], halves[1])
    out_ref[...] = product(spectrum, time_high[...], time_low[...])


def shards(spectra, block_position):
    pairs = spectra.shape[2] // BINS
    view = spectra.reshape(2 * SEGMENTS, pairs, BINS, BLOCK)
    image = pl.pallas_call(
        kernel,
        out_shape=pltpu.VMEM((SLOWNESS // FREQ, LAG_TIMES), jnp.float32),
        in_specs=[
            pl.BlockSpec(memory_space=pl.ANY),
            pl.BlockSpec(memory_space=pl.ANY),
        ],
        out_specs=pl.BlockSpec(memory_space=pltpu.VMEM),
        scratch_shapes=[
            pltpu.SMEM((CHAN,), jnp.int32),
            pltpu.VMEM((CHAN, 2 * SEGMENTS, BINS, BLOCK), jnp.bfloat16),
            pltpu.VMEM((CHAN, 2 * SEGMENTS, BINS, BLOCK), jnp.bfloat16),
            pltpu.VMEM((CHAN, BINS * BLOCK, ROWS), jnp.bfloat16),
            pltpu.VMEM((CHAN, ROWS, 2 * BLOCK), jnp.bfloat16),
            pltpu.VMEM((BINS, CHAN * SLABS, 2 * BLOCK), jnp.float32),
            pltpu.VMEM((BINS, CHAN * SLABS, 2 * BLOCK), jnp.float32),
            pltpu.VMEM((BINS, 4 * BLOCK, BLOCK), jnp.bfloat16),
            pltpu.VMEM((BINS, 4 * BLOCK, BLOCK), jnp.bfloat16),
            pltpu.VMEM((2 * FREQS, LAG_TIMES), jnp.bfloat16),
            pltpu.VMEM((2 * FREQS, LAG_TIMES), jnp.bfloat16),
            pltpu.VMEM((CHAN * SLABS, BLOCK), jnp.float32),
            pltpu.VMEM((CHAN * SLABS, BLOCK), jnp.float32),
            pltpu.VMEM((BINS * BLOCK, 2 * BLOCK), jnp.float32),
            pltpu.VMEM((BINS, CHAN * SLABS, 4 * BLOCK), jnp.float32),
            pltpu.VMEM((CHAN * SLABS, 1, BLOCK), jnp.float32),
            pltpu.VMEM((FREQ * CHAN, 1, BLOCK), jnp.float32),
            pltpu.SemaphoreType.REGULAR,
            pltpu.SemaphoreType.REGULAR,
            pltpu.SemaphoreType.DMA,
            pltpu.SemaphoreType.DMA((CHAN,)),
            pltpu.SemaphoreType.DMA((CHAN,)),
            pltpu.SemaphoreType.DMA((CHAN,)),
            pltpu.SemaphoreType.DMA,
            pltpu.SemaphoreType.DMA,
        ],
        compiler_params=pltpu.CompilerParams(collective_id=0, has_side_effects=True),
        name="slant_stack",
    )(block_position, view)
    return image.reshape(1, image.shape[0], image.shape[1])


def solution(mesh):
    return jax.shard_map(
        shards,
        mesh=mesh,
        in_specs=(P(None, None, "freq", "chan"), P()),
        out_specs=P("chan", "freq", None),
        check_vma=False,
    )
```
